32 devices in a mesh: rep: 2 (over core), ep: 16 (over z, y, x).
Axes of the slice: x: 2, y: 2, z: 4, core: 2. Of those that a mesh axis runs over, the one named last changes fastest.
Arguments:
- first_half: bfloat16 [2048, 2048], P('ep'), may hold values from -6 to 6
- second_half: bfloat16 [2048, 2048], P('ep'), may hold values from -6 to 6
- second_grad: bfloat16 [2048, 2048], P('ep'), may hold values from -3 to 3
- norm_gain: bfloat16 [2048], replicated, may hold values from 0.5 to 1.5
- expert_ids: int32 [2048, 8], P('ep'), may hold values from 0 to 15, all different within a row; in each aligned block of 128 rows (0 to 127, 128 to 255, ...) at most 80 rows name the same one
- gates: float32 [2048, 8], P('ep'), may hold values from 0.02 to 0.3
- w_gate: bfloat16 [16, 2048, 768], P('ep', None, 'rep'), may hold values from -0.125 to 0.125
- w_up: bfloat16 [16, 2048, 768], P('ep', None, 'rep'), may hold values from -0.125 to 0.125
- w_down: bfloat16 [16, 768, 2048], P('ep', 'rep'), may hold values from -0.21875 to 0.21875
Outputs:
- inverted: bfloat16 [2048, 2048], P('ep')
- first_grad: bfloat16 [2048, 2048], P('ep')
- gates_grad: float32 [2048, 8], P('ep')
- w_down_grad: bfloat16 [16, 768, 2048], P('ep', 'rep')
The draws below stay inside these ranges and needn't reach their ends.
Inputs may be any that keep to these rules, and one draw needn't show every extreme that they name: `expert_ids`: the 8 experts of a token are different. Among the tokens of one index of ep (aligned blocks of 128 rows) no expert is named by more than 80 tokens, and in every draw some expert is named by exactly 80 tokens of some block.
All inputs are finite; a program needn't handle non-finite values.
Results may differ from the reference program's by a relative error of at most 0.0072.
Values may be sent and summed in bfloat16 or wider, within the bound.
No kernel may reach another device: no remote copies, remote signals or barrier semaphores. Data moves between devices by JAX's collectives and lax.ppermute only.
A program may use at most 128 MiB of HBM per device.

```python
import math
import jax
import jax.numpy as jnp
import numpy as np
from jax import lax

D = 2048
FF = 768
TOP = 8
TOK_DEV = 128
EXPERTS = 16
TOKENS = 2048
CAP = 80


def shard_levels(rng, dims, pieces, smallest, high):
    def one(dim, parts):
        steps = jax.random.uniform(jax.random.fold_in(jax.random.fold_in(rng, 6), dim), (parts,), jnp.float32, smallest / len(pieces), high / len(pieces))
        return jnp.repeat(jnp.exp(steps), dims[dim] // parts).reshape((-1,) + (1,) * (len(dims) - dim - 1))

    gain = one(*pieces[0])
    for cut in pieces[1:]:
        gain = gain * one(*cut)
    return gain


def routed_block(rng, own, number, rows, number_of, top, bound, lean):
    ranking = jax.random.permutation(rng, number_of)
    packed, ordinary = portions_of(number_of, rows * top, bound, lean, True), portions_of(number_of, rows * top, bound, lean, False)
    places = jnp.arange(number_of)

    def named(sizes, turn):
        used = int((sizes > 0).sum())
        fixed = max(1, used // 4)
        moved = fixed + (places - fixed + turn * (used - fixed)) % max(1, number_of - fixed)
        return jnp.zeros((number_of,), jnp.int32).at[ranking[jnp.where(places < fixed, places, moved)]].set(jnp.asarray(sizes, jnp.int32))

    sizes = jnp.where(number % 4 == 0, named(packed, number // 4), named(ordinary, number - number // 4 - 1))
    mixed = jax.random.permutation(jax.random.fold_in(own, 3), number_of)
    source_of, receiver = mixed[0:number_of // 2 * 2:2], mixed[1:number_of // 2 * 2:2]
    room = jnp.minimum(sizes[source_of] - 1, bound - sizes[receiver]) // 2
    room = jnp.where((source_of == ranking[0]) | (receiver == ranking[0]) | (sizes[receiver] == 0), 0, jnp.maximum(room, 0))
    moved = jax.random.randint(jax.random.fold_in(own, 4), (number_of // 2,), 0, 1 << 20) % (room + 1)
    sizes = sizes.at[source_of].add(-moved).at[receiver].add(moved)
    members = jnp.searchsorted(jnp.cumsum(sizes), jnp.arange(rows * top), side="right").astype(jnp.int32)
    listing = members.reshape(top, rows).T
    listing = listing[jax.random.permutation(jax.random.fold_in(own, 1), rows)]
    turn = jax.random.randint(jax.random.fold_in(own, 2), (rows, 1), 0, top)
    return jnp.take_along_axis(listing, (jnp.arange(top)[None, :] + turn) % top, axis=1)


def portions_of(amount, total, bound, lean, full):
    weights = [(1 << 20) // math.isqrt(standing ** lean) + 1 for standing in range(1, amount + 1)]
    largest = bound if full else min(bound, max(-(-total // amount), total * weights[0] // sum(weights)))
    least = 1 if total - largest >= amount - 1 else 0
    holding, surplus = [largest] + [least] * (amount - 1), total - largest - least * (amount - 1)
    while surplus > 0:
        movable = [i for i in range(1, amount) if holding[i] < largest] or [i for i in range(1, amount) if holding[i] < bound]
        pool, left = sum([weights[i] for i in movable]), surplus
        for i in movable:
            extra = min(bound - holding[i], max(1, left * weights[i] // pool), surplus)
            holding[i] = holding[i] + extra
            surplus = surplus - extra
    return np.array(holding)


def centred(rng, dims, deviation, most, pieces=(), held_as=jnp.bfloat16):
    loudness = shard_levels(rng, dims, pieces, -0.22, 0.18) if pieces else 1.0
    result = jax.random.normal(rng, dims, jnp.float32) * deviation * loudness
    return jnp.minimum(jnp.maximum(result, -most), most).astype(held_as)


def setup_inputs(seed: int = 0) -> dict:
    seeds = jax.random.split(jax.random.key(seed), 10)
    first_half = centred(seeds[0], (TOKENS, D), 1.0, 6.0, ((0, 16),))
    second_half = centred(seeds[1], (TOKENS, D), 1.0, 6.0, ((0, 16),))
    second_grad = centred(seeds[2], (TOKENS, D), 0.5, 3.0, ((0, 16),))
    norm_gain = jnp.clip(1.0 + 0.1 * jax.random.normal(seeds[3], (D,), jnp.float32), 0.5, 1.5).astype(jnp.bfloat16)
    expert_ids_keys = jax.random.split(jax.random.fold_in(seeds[4], 1), TOKENS // TOK_DEV)
    expert_ids_turns = jax.random.permutation(jax.random.fold_in(seeds[4], 3), TOKENS // TOK_DEV)
    expert_ids = jax.vmap(lambda own, number: routed_block(jax.random.fold_in(seeds[4], 2), own, number, TOK_DEV, EXPERTS, TOP, CAP, 2))(expert_ids_keys, expert_ids_turns).reshape((TOKENS, TOP))
    gates = jnp.clip(jnp.exp(math.log(0.3) - 2.7080503 * jax.random.uniform(seeds[5], (TOKENS, TOP), jnp.float32) ** shard_levels(seeds[5], (TOKENS, TOP), ((0, 16),), -0.2, 0.2)), 0.02, 0.3)
    w_gate = centred(seeds[6], (EXPERTS, D, FF), D ** -0.5, 0.125, ((0, 16), (2, 2)))
    w_up = centred(seeds[7], (EXPERTS, D, FF), D ** -0.5, 0.125, ((0, 16), (2, 2)))
    w_down = centred(seeds[8], (EXPERTS, FF, D), FF ** -0.5, 0.21875, ((0, 16), (1, 2)))
    return {"first_half": first_half, "second_half": second_half, "second_grad": second_grad, "norm_gain": norm_gain, "expert_ids": expert_ids, "gates": gates, "w_gate": w_gate, "w_up": w_up, "w_down": w_down}


EPSILON = 1e-06

def contract_rows(left, right):
    return lax.dot_general(left, right, (((0,), (0,)), ((), ())), preferred_element_type=jnp.float32)

def contract_cols(left, right):
    return lax.dot_general(left, right, (((1,), (1,)), ((), ())), preferred_element_type=jnp.float32)

def expert_pass(row_inputs, row_scaled, gate_mat, up_mat, down_mat):
    gate_pre = jnp.dot(row_inputs, gate_mat, preferred_element_type=jnp.float32)
    up_pre = jnp.dot(row_inputs, up_mat, preferred_element_type=jnp.float32)
    sigmoid_gate = jax.nn.sigmoid(gate_pre)
    swish_gate = gate_pre * sigmoid_gate
    hidden = (swish_gate * up_pre).astype(jnp.bfloat16)
    output = jnp.dot(hidden, down_mat, preferred_element_type=jnp.float32)
    hidden_grad = contract_cols(row_scaled, down_mat)
    gate_grad = (hidden_grad * up_pre * sigmoid_gate * (1.0 + gate_pre * (1.0 - sigmoid_gate))).astype(jnp.bfloat16)
    up_grad = (hidden_grad * swish_gate).astype(jnp.bfloat16)
    input_grad = contract_cols(gate_grad, gate_mat) + contract_cols(up_grad, up_mat)
    return (output, input_grad, contract_rows(hidden, row_scaled))

def reference(first_half, second_half, second_grad, norm_gain, expert_ids, gates, w_gate, w_up, w_down):
    tokens_all, model_width = first_half.shape
    top_count = expert_ids.shape[1]
    experts_all = w_gate.shape[0]
    assigned = tokens_all * top_count
    sources = tokens_all // TOK_DEV
    flat_ids = expert_ids.reshape(assigned).astype(jnp.int32)
    block_of = (jnp.arange(assigned, dtype=jnp.int32) // (TOK_DEV * top_count)).astype(jnp.int32)
    sort_keys = block_of * experts_all + flat_ids
    sort_order = jnp.argsort(sort_keys, stable=True).astype(jnp.int32)
    sorted_keys = sort_keys[sort_order]
    first_pos = jnp.searchsorted(sorted_keys, sorted_keys, side='left').astype(jnp.int32)
    rank_in_block = jnp.zeros((assigned,), jnp.int32).at[sort_order].set(jnp.arange(assigned, dtype=jnp.int32) - first_pos)
    per_expert = sources * CAP
    position = flat_ids * per_expert + block_of * CAP + rank_in_block
    slot_table = jnp.full((experts_all * per_expert,), assigned, jnp.int32).at[position].set(jnp.arange(assigned, dtype=jnp.int32))
    slot_table = slot_table.reshape(experts_all, per_expert)
    values = first_half.astype(jnp.float32)
    inverse = lax.rsqrt(lax.optimization_barrier(jnp.mean(values * values, axis=1, keepdims=True)) + EPSILON)
    gain_value = norm_gain.astype(jnp.float32)
    normed = (values * inverse * gain_value).astype(jnp.bfloat16)
    cotangent = second_grad.astype(jnp.float32)
    flat_gates = gates.reshape(assigned)
    zero_half = jnp.zeros((), jnp.bfloat16)

    def per_expert_step(running, inputs):
        sub_total, grad_total, gate_total = running
        index_row, gate_mat, up_mat, down_mat = inputs
        is_live = index_row < assigned
        clamped = jnp.minimum(index_row, assigned - 1)
        token_rows = clamped // top_count
        row_gates = flat_gates[clamped]
        row_inputs = jnp.where(is_live[:, None], normed[token_rows], zero_half)
        row_scaled = jnp.where(is_live[:, None], (row_gates[:, None] * cotangent[token_rows]).astype(jnp.bfloat16), zero_half)
        output, input_grad, grad_down = expert_pass(row_inputs, row_scaled, gate_mat, up_mat, down_mat)
        out_float = lax.optimization_barrier(output.astype(jnp.bfloat16)).astype(jnp.float32)
        grad_float = lax.optimization_barrier(input_grad.astype(jnp.bfloat16)).astype(jnp.float32)
        sub_total = sub_total.at[token_rows].add(jnp.where(is_live[:, None], row_gates[:, None] * out_float, 0.0))
        grad_total = grad_total.at[token_rows].add(jnp.where(is_live[:, None], grad_float, 0.0))
        gate_term = lax.optimization_barrier(jnp.sum(cotangent[token_rows] * out_float, axis=1))
        gate_total = gate_total.at[clamped].add(jnp.where(is_live, gate_term, 0.0))
        return ((sub_total, grad_total, gate_total), grad_down.astype(jnp.bfloat16))
    start = (jnp.zeros((tokens_all, model_width), jnp.float32), jnp.zeros((tokens_all, model_width), jnp.float32), jnp.zeros((assigned,), jnp.float32))
    finals, stacked = lax.scan(per_expert_step, start, (slot_table, w_gate, w_up, w_down))
    sub_total, grad_total, gate_total = finals
    inverted = (second_half.astype(jnp.float32) - sub_total).astype(jnp.bfloat16)
    gates_grad = gate_total.reshape(tokens_all, top_count)
    normed_grad = grad_total * gain_value
    first_grad = (inverse * normed_grad - values * inverse * inverse * inverse * lax.optimization_barrier(jnp.mean(normed_grad * values, axis=1, keepdims=True))).astype(jnp.bfloat16)
    return (inverted, first_grad, gates_grad, stacked)
```

```python
import functools

import jax
import jax.numpy as jnp
from jax import lax
from jax.experimental import pallas as pl
from jax.experimental.pallas import tpu as pltpu
from jax.sharding import PartitionSpec as P

EPSILON = 1e-06
META = 8
LANES = 128


def contract_rows(left, right):
    return lax.dot_general(
        left, right, (((0,), (0,)), ((), ())), preferred_element_type=jnp.float32
    )


def contract_cols(left, right):
    return lax.dot_general(
        left, right, (((1,), (1,)), ((), ())), preferred_element_type=jnp.float32
    )


def product(left, right):
    return jnp.dot(left, right, preferred_element_type=jnp.float32)


def chooser(tile, slots):
    code = tile[0:1, :].astype(jnp.float32)
    number = lax.broadcasted_iota(jnp.int32, (slots, code.shape[1]), 0).astype(jnp.float32)
    return number == code


def one_hot(tile, slots):
    return chooser(tile, slots).astype(jnp.float32).astype(jnp.bfloat16)


def gate_row(tile):
    parts = tile.astype(jnp.float32)
    return parts[1:2, :] + parts[2:3, :] + parts[3:4, :]


def prologue_kernel(half, slots, first, grad, gain, ids, gates, who, block):
    tokens = first.shape[0]
    replica = who[0]

    @pl.when(replica == 0)
    def _():
        values = first[...].astype(jnp.float32)
        inverse = lax.rsqrt(jnp.mean(values * values, axis=1, keepdims=True) + EPSILON)
        block[0:tokens, :] = (values * inverse * gain[...].astype(jnp.float32)).astype(jnp.bfloat16)

    @pl.when(replica != 0)
    def _():
        block[0:tokens, :] = grad[...]

    experts = block.shape[1] // tokens
    expert = lax.broadcasted_iota(jnp.int32, (experts, tokens), 0)
    named = jnp.zeros((experts, tokens), jnp.float32)
    weight = jnp.zeros((experts, tokens), jnp.float32)
    for k in range(ids.shape[0]):
        hit = ids[k : k + 1, :] == expert
        named = named + jnp.where(hit, 1.0, 0.0)
        weight = weight + jnp.where(hit, gates[k : k + 1, :], 0.0)
    before = lax.broadcasted_iota(jnp.int32, (tokens, tokens), 0)
    after = lax.broadcasted_iota(jnp.int32, (tokens, tokens), 1)
    earlier = jnp.where(before < after, 1.0, 0.0).astype(jnp.bfloat16)
    rank = product(named.astype(jnp.bfloat16), earlier)
    rank = rank - (replica * half).astype(jnp.float32)
    rank = jnp.where(rank < 0.0, rank + slots, rank)
    code = jnp.where(named > 0.0, rank, -1.0)
    high = weight.astype(jnp.bfloat16).astype(jnp.float32)
    middle = (weight - high).astype(jnp.bfloat16).astype(jnp.float32)
    low = weight - high - middle
    line = lax.broadcasted_iota(jnp.int32, (META, tokens), 0)
    for e in range(experts):
        tile = jnp.where(line == 0, code[e : e + 1, :], 0.0)
        tile = jnp.where(line == 1, high[e : e + 1, :], tile)
        tile = jnp.where(line == 2, middle[e : e + 1, :], tile)
        tile = jnp.where(line == 3, low[e : e + 1, :], tile)
        block[tokens : tokens + META, e * tokens : (e + 1) * tokens] = tile.astype(jnp.bfloat16)


def pack_kernel(slots, block, who, to_x, to_y, own, routes):
    tokens = block.shape[0] - META
    half = block.shape[1] // 2

    def tile_of(place):
        start = pl.multiple_of(who[place] * tokens, LANES)
        return block[tokens : tokens + META, pl.ds(start, tokens)]

    me, ex, ey, ed = (tile_of(place) for place in range(4))
    end = tokens + slots
    to_x[0:tokens, :] = block[0:tokens, 0:half]
    to_x[tokens:end, :] = product(one_hot(ex, slots), block[0:tokens, half:]).astype(jnp.bfloat16)
    to_x[end : end + META, :] = jnp.zeros((META, half), jnp.bfloat16)
    to_x[end : end + META, 0:tokens] = ex
    to_x[end : end + META, tokens : 2 * tokens] = ed
    to_y[0:tokens, :] = block[0:tokens, half:]
    to_y[tokens:end, :] = product(one_hot(ey, slots), block[0:tokens, 0:half]).astype(jnp.bfloat16)
    to_y[end : end + META, :] = jnp.zeros((META, half), jnp.bfloat16)
    to_y[end : end + META, 0:tokens] = ey
    to_y[end : end + META, tokens : 2 * tokens] = ed
    own[...] = product(one_hot(me, slots), block[0:tokens, :]).astype(jnp.bfloat16)
    routes[0:META, :] = me
    routes[META : 2 * META, :] = ex
    routes[2 * META : 3 * META, :] = ey


def forward_kernel(slots, got_x, got_y, on_y, on_x, mine_x, mine_y):
    tokens = got_x.shape[0] - slots - META
    end = tokens + slots
    half = got_x.shape[1]
    for got, on, mine in ((got_x, on_y, mine_x), (got_y, on_x, mine_y)):
        me = got[end : end + META, 0:tokens]
        other = got[end : end + META, tokens : 2 * tokens]
        rows = got[0:tokens, :]
        on[0:slots, :] = product(one_hot(other, slots), rows).astype(jnp.bfloat16)
        on[slots : slots + META, :] = jnp.zeros((META, half), jnp.bfloat16)
        on[slots : slots + META, 0:tokens] = other
        mine[...] = product(one_hot(me, slots), rows).astype(jnp.bfloat16)


def gather_kernel(slots, own, got_x, got_y, mine_x, mine_y, by_y, by_x, keep, send):
    portion = slots // 2
    tokens = got_x.shape[0] - slots - META
    half = got_x.shape[1]
    for base, out in ((0, keep), (portion, send)):
        rows = slice(base, base + portion)
        late = slice(tokens + base, tokens + base + portion)
        out[0:portion, :] = own[rows, :]
        out[portion : 2 * portion, 0:half] = mine_x[rows, :]
        out[portion : 2 * portion, half:] = got_x[late, :]
        out[2 * portion : 3 * portion, 0:half] = got_y[late, :]
        out[2 * portion : 3 * portion, half:] = mine_y[rows, :]
        out[3 * portion : 4 * portion, 0:half] = by_y[rows, :]
        out[3 * portion : 4 * portion, half:] = by_x[rows, :]


def expert_kernel(
    keep, got, routes, got_x, got_y, by_y, who, g0, u0, d0, g1, u1, d1,
    keep_out, send_out, factor, scaled_out, hidden_out, vg0, vu0, vd0, vg1, vu1, vd1, arrive,
):
    replica = who[0]
    portion = keep.shape[0] // 4
    tokens = routes.shape[1]
    copies = []
    for i, (source, held) in enumerate(
        ((g0, vg0), (u0, vu0), (g1, vg1), (u1, vu1), (d0, vd0), (d1, vd1))
    ):
        copy = pltpu.make_async_copy(source, held, arrive.at[i])
        copy.start()
        copies.append(copy)
    is_first = replica == 0
    inputs = jnp.where(is_first, keep[...], got[...])
    grads = jnp.where(is_first, got[...], keep[...])
    end = got_x.shape[0] - META
    tiles = (
        routes[0:META, :],
        got_x[end : end + META, 0:tokens],
        got_y[end : end + META, 0:tokens],
        by_y[by_y.shape[0] - META : by_y.shape[0], 0:tokens],
    )
    choices = [chooser(tile, portion) for tile in tiles]
    gate = jnp.concatenate(
        [
            jnp.sum(jnp.where(c, gate_row(tile), 0.0), axis=1, keepdims=True)
            for c, tile in zip(choices, tiles)
        ],
        axis=0,
    )
    scaled = (gate * grads.astype(jnp.float32)).astype(jnp.bfloat16)
    scaled_out[...] = scaled
    width = g0.shape[1]
    pres = []
    for i, (gate_mat, up_mat) in enumerate(((vg0, vu0), (vg1, vu1))):
        copies[2 * i].wait()
        copies[2 * i + 1].wait()
        pres.append((product(inputs, gate_mat[...]), product(inputs, up_mat[...])))
    output, input_grad = None, None
    for i, (gate_mat, up_mat, down_mat) in enumerate(((vg0, vu0, vd0), (vg1, vu1, vd1))):
        gate_pre, up_pre = pres[i]
        sigmoid_gate = jax.nn.sigmoid(gate_pre)
        swish_gate = gate_pre * sigmoid_gate
        hidden = (swish_gate * up_pre).astype(jnp.bfloat16)
        hidden_out[:, i * width : (i + 1) * width] = hidden
        copies[4 + i].wait()
        hidden_grad = contract_cols(scaled, down_mat[...])
        gate_grad = (
            hidden_grad * up_pre * sigmoid_gate * (1.0 + gate_pre * (1.0 - sigmoid_gate))
        ).astype(jnp.bfloat16)
        up_grad = (hidden_grad * swish_gate).astype(jnp.bfloat16)
        part = product(hidden, down_mat[...])
        back = contract_cols(gate_grad, gate_mat[...]) + contract_cols(up_grad, up_mat[...])
        output = part if output is None else output + part
        input_grad = back if input_grad is None else input_grad + back
    rounded = output.astype(jnp.bfloat16).astype(jnp.float32)
    inner = jnp.sum(grads.astype(jnp.float32) * rounded, axis=1, keepdims=True)
    weighted = (gate * rounded).astype(jnp.bfloat16)
    rounded_grad = input_grad.astype(jnp.bfloat16)
    keep_out[...] = jnp.where(is_first, weighted, rounded_grad)
    send_out[...] = jnp.where(is_first, rounded_grad, weighted)
    for i, choice in enumerate(choices):
        part = inner[i * portion : (i + 1) * portion, :]
        factor[i : i + 1, :] = jnp.sum(jnp.where(choice, part, 0.0), axis=0, keepdims=True)
    factor[4:8, :] = jnp.zeros((4, tokens), jnp.float32)


def corner_kernel(keep, got, on_y, on_x):
    portion = keep.shape[0]
    half = on_y.shape[1]
    on_y[0:portion, :] = keep[:, 0:half]
    on_y[portion:, :] = got[:, 0:half]
    on_x[0:portion, :] = keep[:, half:]
    on_x[portion:, :] = got[:, half:]


def both(keep, got, number, portion):
    rows = slice(number * portion, (number + 1) * portion)
    return jnp.concatenate([keep[rows, :], got[rows, :]], axis=0)


def return_kernel(slots, keep, got, got_x, got_y, from_x, from_y, to_x, to_y):
    portion = slots // 2
    half = to_x.shape[1]
    tokens = to_x.shape[0] - slots
    end = tokens + slots
    for number, route, corner, to, dense, compact in (
        (1, got_x, from_y, to_x, slice(0, half), slice(half, 2 * half)),
        (2, got_y, from_x, to_y, slice(half, 2 * half), slice(0, half)),
    ):
        rows = both(keep, got, number, portion)
        me = route[end : end + META, 0:tokens]
        other = route[end : end + META, tokens : 2 * tokens]
        total = contract_rows(one_hot(me, slots), rows[:, dense])
        total = total + contract_rows(one_hot(other, slots), corner[...])
        to[0:tokens, :] = total.astype(jnp.bfloat16)
        to[tokens:end, :] = rows[:, compact]


def plane_sum(slots, keep, got, routes, from_x, from_y):
    half = from_x.shape[1]
    tokens = from_x.shape[0] - slots
    rows = both(keep, got, 0, slots // 2)
    me, ex, ey = (one_hot(routes[i * META : (i + 1) * META, :], slots) for i in range(3))
    mine = contract_rows(me, rows)
    left = from_x[0:tokens, :].astype(jnp.float32) + contract_rows(ey, from_y[tokens:, :])
    right = from_y[0:tokens, :].astype(jnp.float32) + contract_rows(ex, from_x[tokens:, :])
    return mine[:, 0:half] + left, mine[:, half:] + right


def plane_kernel(slots, keep, got, routes, from_x, from_y, *rest):
    total = rest[-1]
    half = from_x.shape[1]
    left, right = plane_sum(slots, keep, got, routes, from_x, from_y)
    for extra in rest[:-1]:
        left = left + extra[:, 0:half].astype(jnp.float32)
        right = right + extra[:, half:].astype(jnp.float32)
    total[:, 0:half] = left.astype(jnp.bfloat16)
    total[:, half:] = right.astype(jnp.bfloat16)


def last_kernel(slots, keep, got, routes, from_x, from_y, add_a, add_b, first, second, gain, who, out):
    half = from_x.shape[1]
    left, right = plane_sum(slots, keep, got, routes, from_x, from_y)
    total = jnp.concatenate([left, right], axis=1)
    total = total + add_a[...].astype(jnp.float32) + add_b[...].astype(jnp.float32)

    @pl.when(who[0] == 0)
    def _():
        out[...] = (second[...].astype(jnp.float32) - total).astype(jnp.bfloat16)

    @pl.when(who[0] != 0)
    def _():
        values = first[...].astype(jnp.float32)
        inverse = lax.rsqrt(jnp.mean(values * values, axis=1, keepdims=True) + EPSILON)
        normed_grad = total * gain[...].astype(jnp.float32)
        inner = jnp.mean(normed_grad * values, axis=1, keepdims=True)
        out[...] = (
            inverse * normed_grad - values * inverse * inverse * inverse * inner
        ).astype(jnp.bfloat16)


def call(kernel, name, outs, args, scalars=(), hbm=(), scratch=()):
    specs = []
    for i in range(len(args)):
        if i in scalars:
            specs.append(pl.BlockSpec(memory_space=pltpu.SMEM))
        elif i in hbm:
            specs.append(pl.BlockSpec(memory_space=pl.ANY))
        else:
            specs.append(pl.BlockSpec(memory_space=pltpu.VMEM))
    return pl.pallas_call(
        kernel,
        out_shape=[jax.ShapeDtypeStruct(shape, dtype) for shape, dtype in outs],
        in_specs=specs,
        out_specs=[pl.BlockSpec(memory_space=pltpu.VMEM)] * len(outs),
        scratch_shapes=list(scratch),
        name=name,
    )(*args)


def dense_local(first_half, second_half, second_grad, norm_gain, expert_ids, gates, w_gate, w_up, w_down):
    tokens, width = first_half.shape
    half = width // 2
    owners = lax.axis_size("ep")
    replica = lax.axis_index("rep").astype(jnp.int32)
    place = lax.axis_index("ep").astype(jnp.int32)
    top = expert_ids.shape[1]
    slots = 5 * tokens * top // (4 * owners)
    portion = slots // 2
    plane = 4
    line = owners // plane
    bf16, f32 = jnp.bfloat16, jnp.float32

    def steps(move):
        pairs = [(i, move(i // plane)) for i in range(owners)]
        return [(i, to * plane + i % plane) for i, to in pairs if to is not None]

    across_x = [(i, i ^ 1) for i in range(owners)]
    across_y = [(i, i ^ 2) for i in range(owners)]
    pairs = steps(lambda z: z ^ 1)
    middle = steps({1: 2, 2: 1}.get)
    outward = steps({1: 0, 2: 3}.get)
    inward = steps({0: 1, 3: 2}.get)
    swap = [(0, 1), (1, 0)]

    def shift(value, route):
        return lax.ppermute(value, "ep", route)

    def other(value):
        return lax.ppermute(value, "rep", swap)

    z = place // plane
    is_middle = (z > 0) & (z < line - 1)
    who_rep = replica.reshape(1)
    who = jnp.stack([place, place ^ 1, place ^ 2, place ^ 3])
    gain = norm_gain.reshape(1, width)
    gate0, up0, down0 = w_gate[0], w_up[0], w_down[0]
    hidden_units = gate0.shape[1]

    with jax.named_scope("prologue"):
        (block,) = call(
            functools.partial(prologue_kernel, portion, slots),
            "prologue",
            [((tokens + META, width), bf16)],
            [first_half, second_grad, gain, expert_ids.T, gates.T, who_rep],
            scalars=(5,),
        )
    near = shift(block, pairs)
    mid_b = shift(block, middle)
    mid_c = shift(near, middle)
    end_b = shift(mid_b, outward)
    end_c = shift(mid_c, outward)
    gate1, up1, down1 = other(gate0), other(up0), other(down0)
    blocks = (
        block,
        near,
        jnp.where(is_middle, mid_b, end_b),
        jnp.where(is_middle, mid_c, end_c),
    )

    def dispatch(value):
        to_x, to_y, own, routes = call(
            functools.partial(pack_kernel, slots),
            "pack",
            [
                ((tokens + slots + META, half), bf16),
                ((tokens + slots + META, half), bf16),
                ((slots, width), bf16),
                ((3 * META, tokens), bf16),
            ],
            [value, who],
            scalars=(1,),
        )
        got_x, got_y = shift(to_x, across_x), shift(to_y, across_y)
        on_y, on_x, mine_x, mine_y = call(
            functools.partial(forward_kernel, slots),
            "forward",
            [((slots + META, half), bf16)] * 2 + [((slots, half), bf16)] * 2,
            [got_x, got_y],
        )
        by_y, by_x = shift(on_y, across_y), shift(on_x, across_x)
        keep, send = call(
            functools.partial(gather_kernel, slots),
            "gather",
            [((4 * portion, width), bf16)] * 2,
            [own, got_x, got_y, mine_x, mine_y, by_y, by_x],
        )
        return keep, other(send), routes, got_x, got_y, by_y

    def experts(keep, got, routes, got_x, got_y, by_y):
        rows = 4 * portion
        return call(
            expert_kernel,
            "experts",
            [
                ((rows, width), bf16),
                ((rows, width), bf16),
                ((8, tokens), f32),
                ((rows, width), bf16),
                ((rows, 2 * hidden_units), bf16),
            ],
            [keep, got, routes, got_x, got_y, by_y, who_rep, gate0, up0, down0, gate1, up1, down1],
            scalars=(6,),
            hbm=(7, 8, 9, 10, 11, 12),
            scratch=[
                pltpu.VMEM((width, hidden_units), bf16),
                pltpu.VMEM((width, hidden_units), bf16),
                pltpu.VMEM((hidden_units, width), bf16),
            ]
            * 2
            + [pltpu.SemaphoreType.DMA((6,))],
        )

    arrived = [dispatch(value) for value in blocks]
    solved = [experts(*a) for a in arrived]

    def give_back(a, s):
        keep, got = s[0], other(s[1])
        on_y, on_x = pl.pallas_call(
            corner_kernel,
            grid=(1,),
            out_shape=[jax.ShapeDtypeStruct((slots, half), bf16)] * 2,
            in_specs=[pl.BlockSpec((portion, width), lambda i: (3, 0))] * 2,
            out_specs=[pl.BlockSpec((slots, half), lambda i: (0, 0))] * 2,
            name="corner",
        )(keep, got)
        from_y, from_x = shift(on_y, across_y), shift(on_x, across_x)
        to_x, to_y = call(
            functools.partial(return_kernel, slots),
            "giveback",
            [((tokens + slots, half), bf16)] * 2,
            [keep, got, a[3], a[4], from_x, from_y],
        )
        return [keep, got, a[2], shift(to_x, across_x), shift(to_y, across_y)]

    def plane_total(parts, *extra):
        return call(
            functools.partial(plane_kernel, slots),
            "plane",
            [((tokens, width), bf16)],
            [*parts, *extra],
        )[0]

    def added(a, b):
        return (a.astype(f32) + b.astype(f32)).astype(bf16)

    total_c = plane_total(give_back(arrived[3], solved[3]))
    total_c = added(total_c, shift(total_c, inward))
    through_c = shift(total_c, middle)
    total_b = plane_total(give_back(arrived[2], solved[2]))
    total_b = added(total_b, shift(total_b, inward))
    through_b = shift(total_b, middle)
    total_a = plane_total(give_back(arrived[1], solved[1]), through_c)
    through_a = shift(total_a, pairs)
    parts = give_back(arrived[0], solved[0])
    (mine,) = call(
        functools.partial(last_kernel, slots),
        "last",
        [((tokens, width), bf16)],
        [*parts, through_a, through_b, first_half, second_half, gain, who_rep],
        scalars=(10,),
    )
    theirs = other(mine)
    is_first = replica == 0
    inverted = jnp.where(is_first, mine, theirs)
    first_grad = jnp.where(is_first, theirs, mine)

    scaled = jnp.concatenate([s[3] for s in solved], axis=0)
    hidden = jnp.concatenate([s[4] for s in solved], axis=0)
    down_theirs = contract_rows(hidden[:, hidden_units:], scaled)
    down_mine = contract_rows(hidden[:, :hidden_units], scaled) + other(down_theirs)
    w_down_grad = down_mine.astype(bf16)[None]

    factors = jnp.stack([s[2][:plane] for s in solved]).reshape(owners, tokens)
    target = jnp.arange(owners, dtype=jnp.int32)
    target_z = target // plane
    upper = z >= line // 2
    set_c = jnp.where(upper, 0, line - 1)
    set_b = jnp.where(upper, 1, line - 2)
    kind = jnp.where(
        target_z == z, 0, jnp.where(target_z == z ^ 1, 1, jnp.where(target_z == set_b, 2, 3))
    )
    del set_c
    source = kind * plane + (target % plane ^ place % plane)
    pick = source[:, None] == target[None, :]
    ordered = jnp.sum(jnp.where(pick[:, :, None], factors[None], 0.0), axis=1)
    by_expert = lax.all_to_all(ordered, "ep", split_axis=0, concat_axis=0, tiled=True)
    by_expert = by_expert + other(by_expert)
    asked = expert_ids[:, :, None] == jnp.arange(owners, dtype=jnp.int32)[None, None, :]
    gates_grad = jnp.sum(jnp.where(asked, by_expert.T[:, None, :], 0.0), axis=2)
    return (inverted, first_grad, gates_grad, w_down_grad)


def expert_pass(row_inputs, row_scaled, gate_mat, up_mat, down_mat):
    gate_pre = jnp.dot(row_inputs, gate_mat, preferred_element_type=jnp.float32)
    up_pre = jnp.dot(row_inputs, up_mat, preferred_element_type=jnp.float32)
    sigmoid_gate = jax.nn.sigmoid(gate_pre)
    swish_gate = gate_pre * sigmoid_gate
    hidden = (swish_gate * up_pre).astype(jnp.bfloat16)
    output = jnp.dot(hidden, down_mat, preferred_element_type=jnp.float32)
    hidden_grad = contract_cols(row_scaled, down_mat)
    gate_grad = (
        hidden_grad * up_pre * sigmoid_gate * (1.0 + gate_pre * (1.0 - sigmoid_gate))
    ).astype(jnp.bfloat16)
    up_grad = (hidden_grad * swish_gate).astype(jnp.bfloat16)
    input_grad = contract_cols(gate_grad, gate_mat) + contract_cols(up_grad, up_mat)
    return (output, input_grad, contract_rows(hidden, row_scaled))


def local(first_half, second_half, second_grad, norm_gain, expert_ids, gates, w_gate, w_up, w_down):
    token_count, model_width = first_half.shape
    top_count = expert_ids.shape[1]
    local_experts = w_gate.shape[0]
    owners = lax.axis_size("ep")
    replicas = lax.axis_size("rep")
    replica_index = lax.axis_index("rep")
    experts_all = local_experts * owners
    assigned = token_count * top_count
    capacity = 5 * token_count * top_count // (4 * experts_all)
    portion = capacity // replicas
    slots_all = experts_all * capacity
    slots_mine = experts_all * portion
    full_gate, full_up, full_down = (
        lax.all_gather(w_gate, "rep", axis=2, tiled=True),
        lax.all_gather(w_up, "rep", axis=2, tiled=True),
        lax.all_gather(w_down, "rep", axis=1, tiled=True),
    )
    expert_range = jnp.arange(experts_all, dtype=jnp.int32)
    hits = (expert_ids[:, :, None] == expert_range[None, None, :]).astype(jnp.bfloat16)
    incidence = jnp.sum(hits, axis=1)
    token_range = jnp.arange(token_count, dtype=jnp.int32)
    strictly_before = (token_range[:, None] > token_range[None, :]).astype(jnp.bfloat16)
    earlier = jnp.dot(strictly_before, incidence, preferred_element_type=jnp.float32)
    slot_rank = jnp.sum(hits.astype(jnp.float32) * earlier[:, None, :], axis=2).astype(jnp.int32)
    flat_ids = expert_ids.reshape(assigned)
    flat_rank = slot_rank.reshape(assigned)
    target = flat_ids * capacity + flat_rank
    local_rank = flat_rank - replica_index * portion
    is_mine = (local_rank >= 0) & (local_rank < portion)
    destination = jnp.where(is_mine, flat_ids * portion + local_rank, slots_mine)
    slot_source = (
        jnp.full((slots_mine,), assigned, jnp.int32)
        .at[destination]
        .set(jnp.arange(assigned, dtype=jnp.int32), mode="drop")
    )
    is_live = slot_source < assigned
    clamped = jnp.minimum(slot_source, assigned - 1)
    source_token = clamped // top_count
    values = first_half.astype(jnp.float32)
    inverse = lax.rsqrt(jnp.mean(values * values, axis=1, keepdims=True) + EPSILON)
    gain_value = norm_gain.astype(jnp.float32)
    normed = (values * inverse * gain_value).astype(jnp.bfloat16)
    flat_gates = gates.reshape(assigned)
    zero_half = jnp.zeros((), jnp.bfloat16)
    mine_inputs = jnp.where(is_live[:, None], normed[source_token], zero_half)
    slot_scaled = (
        flat_gates[clamped][:, None] * second_grad[source_token].astype(jnp.float32)
    ).astype(jnp.bfloat16)
    mine_scaled = jnp.where(is_live[:, None], slot_scaled, zero_half)
    got_inputs, got_scaled = (
        lax.all_to_all(mine_inputs, "ep", split_axis=0, concat_axis=0, tiled=True),
        lax.all_to_all(mine_scaled, "ep", split_axis=0, concat_axis=0, tiled=True),
    )
    grouped_inputs = got_inputs.reshape(owners, local_experts, portion, model_width)
    grouped_scaled = got_scaled.reshape(owners, local_experts, portion, model_width)
    out_list, grad_list, down_list = ([], [], [])
    row_inputs = grouped_inputs[:, 0].reshape(owners * portion, model_width)
    row_scaled = grouped_scaled[:, 0].reshape(owners * portion, model_width)
    output, input_grad, grad_down = expert_pass(
        row_inputs, row_scaled, full_gate[0], full_up[0], full_down[0]
    )
    out_list.append(output.astype(jnp.bfloat16).reshape(owners, 1, portion, model_width))
    grad_list.append(input_grad.astype(jnp.bfloat16).reshape(owners, 1, portion, model_width))
    down_list.append(grad_down)
    back_out = out_list[0].reshape(owners * local_experts * portion, model_width)
    back_grad = grad_list[0].reshape(owners * local_experts * portion, model_width)
    summed_down = lax.psum_scatter(jnp.stack(down_list), "rep", scatter_dimension=1, tiled=True)
    w_down_grad = summed_down.astype(jnp.bfloat16)
    returned_out, returned_grad = (
        lax.all_to_all(back_out, "ep", split_axis=0, concat_axis=0, tiled=True),
        lax.all_to_all(back_grad, "ep", split_axis=0, concat_axis=0, tiled=True),
    )
    whole_out, whole_grad = (
        lax.all_gather(
            returned_out.reshape(experts_all, portion, model_width), "rep", axis=1, tiled=True
        ),
        lax.all_gather(
            returned_grad.reshape(experts_all, portion, model_width), "rep", axis=1, tiled=True
        ),
    )
    whole_out = whole_out.reshape(slots_all, model_width)
    whole_grad = whole_grad.reshape(slots_all, model_width)
    out_rows = whole_out[target].reshape(token_count, top_count, model_width)
    grad_rows = whole_grad[target].reshape(token_count, top_count, model_width)
    inverted = (
        second_half.astype(jnp.float32)
        - jnp.sum(gates[:, :, None] * out_rows.astype(jnp.float32), axis=1)
    ).astype(jnp.bfloat16)
    gates_grad = jnp.einsum("td,tkd->tk", second_grad, out_rows, preferred_element_type=jnp.float32)
    normed_grad = jnp.sum(grad_rows.astype(jnp.float32), axis=1) * gain_value
    first_grad = (
        inverse * normed_grad
        - values
        * inverse
        * inverse
        * inverse
        * jnp.mean(normed_grad * values, axis=1, keepdims=True)
    ).astype(jnp.bfloat16)
    return (inverted, first_grad, gates_grad, w_down_grad)


def is_dense(mesh, args):
    first_half, expert_ids, w_gate = args[0], args[4], args[6]
    owners, replicas = mesh.shape["ep"], mesh.shape["rep"]
    tokens, width = first_half.shape[0] // owners, first_half.shape[1]
    experts, top = w_gate.shape[0], expert_ids.shape[1]
    slots = 5 * tokens * top // (4 * experts)
    fits = tokens % LANES == 0 and width == experts * tokens and slots % (8 * replicas) == 0
    return fits and experts == owners == 16 and replicas == 2 and 2 * top >= experts


def solution(mesh):
    def run(*args):
        body = dense_local if is_dense(mesh, args) else local
        return jax.shard_map(
            body,
            mesh=mesh,
            in_specs=(
                P("ep", None),
                P("ep", None),
                P("ep", None),
                P(),
                P("ep", None),
                P("ep", None),
                P("ep", None, "rep"),
                P("ep", None, "rep"),
                P("ep", "rep", None),
            ),
            out_specs=(P("ep", None), P("ep", None), P("ep", None), P("ep", "rep", None)),
            check_vma=False,
        )(*args)

    return run
```

```python
import functools

import jax
import jax.numpy as jnp
from jax import lax
from jax.experimental import pallas as pl
from jax.experimental.pallas import tpu as pltpu
from jax.sharding import PartitionSpec as P

EPSILON = 1e-06
META = 8
LANES = 128


def contract_rows(left, right):
    return lax.dot_general(
        left, right, (((0,), (0,)), ((), ())), preferred_element_type=jnp.float32
    )


def contract_cols(left, right):
    return lax.dot_general(
        left, right, (((1,), (1,)), ((), ())), preferred_element_type=jnp.float32
    )


def product(left, right):
    return jnp.dot(left, right, preferred_element_type=jnp.float32)


def chooser(tile, slots):
    code = tile[0:1, :].astype(jnp.float32)
    number = lax.broadcasted_iota(jnp.int32, (slots, code.shape[1]), 0).astype(jnp.float32)
    return number == code


def one_hot(tile, slots):
    return chooser(tile, slots).astype(jnp.float32).astype(jnp.bfloat16)


def gate_row(tile):
    parts = tile.astype(jnp.float32)
    return parts[1:2, :] + parts[2:3, :] + parts[3:4, :]


def prologue_kernel(half, slots, first, grad, gain, ids, gates, who, block):
    tokens = first.shape[0]
    replica = who[0]

    @pl.when(replica == 0)
    def _():
        values = first[...].astype(jnp.float32)
        inverse = lax.rsqrt(jnp.mean(values * values, axis=1, keepdims=True) + EPSILON)
        block[0:tokens, :] = (values * inverse * gain[...].astype(jnp.float32)).astype(jnp.bfloat16)

    @pl.when(replica != 0)
    def _():
        block[0:tokens, :] = grad[...]

    experts = block.shape[1] // tokens
    expert = lax.broadcasted_iota(jnp.int32, (experts, tokens), 0)
    named = jnp.zeros((experts, tokens), jnp.float32)
    weight = jnp.zeros((experts, tokens), jnp.float32)
    for k in range(ids.shape[0]):
        hit = ids[k : k + 1, :] == expert
        named = named + jnp.where(hit, 1.0, 0.0)
        weight = weight + jnp.where(hit, gates[k : k + 1, :], 0.0)
    before = lax.broadcasted_iota(jnp.int32, (tokens, tokens), 0)
    after = lax.broadcasted_iota(jnp.int32, (tokens, tokens), 1)
    earlier = jnp.where(before < after, 1.0, 0.0).astype(jnp.bfloat16)
    rank = product(named.astype(jnp.bfloat16), earlier)
    rank = rank - (replica * half).astype(jnp.float32)
    rank = jnp.where(rank < 0.0, rank + slots, rank)
    code = jnp.where(named > 0.0, rank, -1.0)
    high = weight.astype(jnp.bfloat16).astype(jnp.float32)
    middle = (weight - high).astype(jnp.bfloat16).astype(jnp.float32)
    low = weight - high - middle
    line = lax.broadcasted_iota(jnp.int32, (META, tokens), 0)
    for e in range(experts):
        tile = jnp.where(line == 0, code[e : e + 1, :], 0.0)
        tile = jnp.where(line == 1, high[e : e + 1, :], tile)
        tile = jnp.where(line == 2, middle[e : e + 1, :], tile)
        tile = jnp.where(line == 3, low[e : e + 1, :], tile)
        block[tokens : tokens + META, e * tokens : (e + 1) * tokens] = tile.astype(jnp.bfloat16)


def pack_kernel(slots, block, who, to_x, to_y, own, routes):
    tokens = block.shape[0] - META
    half = block.shape[1] // 2

    def tile_of(place):
        start = pl.multiple_of(who[place] * tokens, LANES)
        return block[tokens : tokens + META, pl.ds(start, tokens)]

    me, ex, ey, ed = (tile_of(place) for place in range(4))
    end = tokens + slots
    to_x[0:tokens, :] = block[0:tokens, 0:half]
    to_x[tokens:end, :] = product(one_hot(ex, slots), block[0:tokens, half:]).astype(jnp.bfloat16)
    to_x[end : end + META, :] = jnp.zeros((META, half), jnp.bfloat16)
    to_x[end : end + META, 0:tokens] = ex
    to_x[end : end + META, tokens : 2 * tokens] = ed
    to_y[0:tokens, :] = block[0:tokens, half:]
    to_y[tokens:end, :] = product(one_hot(ey, slots), block[0:tokens, 0:half]).astype(jnp.bfloat16)
    to_y[end : end + META, :] = jnp.zeros((META, half), jnp.bfloat16)
    to_y[end : end + META, 0:tokens] = ey
    to_y[end : end + META, tokens : 2 * tokens] = ed
    own[...] = product(one_hot(me, slots), block[0:tokens, :]).astype(jnp.bfloat16)
    routes[0:META, :] = me
    routes[META : 2 * META, :] = ex
    routes[2 * META : 3 * META, :] = ey


def forward_kernel(slots, got_x, got_y, on_y, on_x, mine_x, mine_y):
    tokens = got_x.shape[0] - slots - META
    end = tokens + slots
    half = got_x.shape[1]
    for got, on, mine in ((got_x, on_y, mine_x), (got_y, on_x, mine_y)):
        me = got[end : end + META, 0:tokens]
        other = got[end : end + META, tokens : 2 * tokens]
        rows = got[0:tokens, :]
        on[0:slots, :] = product(one_hot(other, slots), rows).astype(jnp.bfloat16)
        on[slots : slots + META, :] = jnp.zeros((META, half), jnp.bfloat16)
        on[slots : slots + META, 0:tokens] = other
        mine[...] = product(one_hot(me, slots), rows).astype(jnp.bfloat16)


def gather_kernel(slots, own, got_x, got_y, mine_x, mine_y, by_y, by_x, keep, send):
    portion = slots // 2
    tokens = got_x.shape[0] - slots - META
    half = got_x.shape[1]
    for base, out in ((0, keep), (portion, send)):
        rows = slice(base, base + portion)
        late = slice(tokens + base, tokens + base + portion)
        out[0:portion, :] = own[rows, :]
        out[portion : 2 * portion, 0:half] = mine_x[rows, :]
        out[portion : 2 * portion, half:] = got_x[late, :]
        out[2 * portion : 3 * portion, 0:half] = got_y[late, :]
        out[2 * portion : 3 * portion, half:] = mine_y[rows, :]
        out[3 * portion : 4 * portion, 0:half] = by_y[rows, :]
        out[3 * portion : 4 * portion, half:] = by_x[rows, :]


def expert_kernel(
    keep, got, routes, got_x, got_y, by_y, who, g0, u0, d0, g1, u1, d1,
    keep_out, send_out, factor, scaled_out, hidden_out, vg0, vu0, vd0, vg1, vu1, vd1, arrive,
):
    replica = who[0]
    portion = keep.shape[0] // 4
    tokens = routes.shape[1]
    copies = []
    for i, (source, held) in enumerate(
        ((g0, vg0), (u0, vu0), (g1, vg1), (u1, vu1), (d0, vd0), (d1, vd1))
    ):
        copy = pltpu.make_async_copy(source, held, arrive.at[i])
        copy.start()
        copies.append(copy)
    is_first = replica == 0
    inputs = jnp.where(is_first, keep[...], got[...])
    grads = jnp.where(is_first, got[...], keep[...])
    end = got_x.shape[0] - META
    tiles = (
        routes[0:META, :],
        got_x[end : end + META, 0:tokens],
        got_y[end : end + META, 0:tokens],
        by_y[by_y.shape[0] - META : by_y.shape[0], 0:tokens],
    )
    choices = [chooser(tile, portion) for tile in tiles]
    gate = jnp.concatenate(
        [
            jnp.sum(jnp.where(c, gate_row(tile), 0.0), axis=1, keepdims=True)
            for c, tile in zip(choices, tiles)
        ],
        axis=0,
    )
    scaled = (gate * grads.astype(jnp.float32)).astype(jnp.bfloat16)
    scaled_out[...] = scaled
    width = g0.shape[1]
    pres = []
    for i, (gate_mat, up_mat) in enumerate(((vg0, vu0), (vg1, vu1))):
        copies[2 * i].wait()
        copies[2 * i + 1].wait()
        pres.append((product(inputs, gate_mat[...]), product(inputs, up_mat[...])))
    output, input_grad = None, None
    for i, (gate_mat, up_mat, down_mat) in enumerate(((vg0, vu0, vd0), (vg1, vu1, vd1))):
        gate_pre, up_pre = pres[i]
        sigmoid_gate = jax.nn.sigmoid(gate_pre)
        swish_gate = gate_pre * sigmoid_gate
        hidden = (swish_gate * up_pre).astype(jnp.bfloat16)
        hidden_out[:, i * width : (i + 1) * width] = hidden
        copies[4 + i].wait()
        hidden_grad = contract_cols(scaled, down_mat[...])
        gate_grad = (
            hidden_grad * up_pre * sigmoid_gate * (1.0 + gate_pre * (1.0 - sigmoid_gate))
        ).astype(jnp.bfloat16)
        up_grad = (hidden_grad * swish_gate).astype(jnp.bfloat16)
        part = product(hidden, down_mat[...])
        back = contract_cols(gate_grad, gate_mat[...]) + contract_cols(up_grad, up_mat[...])
        output = part if output is None else output + part
        input_grad = back if input_grad is None else input_grad + back
    rounded = output.astype(jnp.bfloat16).astype(jnp.float32)
    inner = jnp.sum(grads.astype(jnp.float32) * rounded, axis=1, keepdims=True)
    weighted = (gate * rounded).astype(jnp.bfloat16)
    rounded_grad = input_grad.astype(jnp.bfloat16)
    keep_out[...] = jnp.where(is_first, weighted, rounded_grad)
    send_out[...] = jnp.where(is_first, rounded_grad, weighted)
    for i, choice in enumerate(choices):
        part = inner[i * portion : (i + 1) * portion, :]
        factor[i : i + 1, :] = jnp.sum(jnp.where(choice, part, 0.0), axis=0, keepdims=True)
    factor[4:8, :] = jnp.zeros((4, tokens), jnp.float32)


def corner_kernel(keep, got, on_y, on_x):
    portion = keep.shape[0]
    half = on_y.shape[1]
    on_y[0:portion, :] = keep[:, 0:half]
    on_y[portion:, :] = got[:, 0:half]
    on_x[0:portion, :] = keep[:, half:]
    on_x[portion:, :] = got[:, half:]


def both(keep, got, number, portion):
    rows = slice(number * portion, (number + 1) * portion)
    return jnp.concatenate([keep[rows, :], got[rows, :]], axis=0)


def return_kernel(slots, keep, got, got_x, got_y, from_x, from_y, to_x, to_y):
    portion = slots // 2
    half = to_x.shape[1]
    tokens = to_x.shape[0] - slots
    end = tokens + slots
    for number, route, corner, to, dense, compact in (
        (1, got_x, from_y, to_x, slice(0, half), slice(half, 2 * half)),
        (2, got_y, from_x, to_y, slice(half, 2 * half), slice(0, half)),
    ):
        rows = both(keep, got, number, portion)
        me = route[end : end + META, 0:tokens]
        other = route[end : end + META, tokens : 2 * tokens]
        total = contract_rows(one_hot(me, slots), rows[:, dense])
        total = total + contract_rows(one_hot(other, slots), corner[...])
        to[0:tokens, :] = total.astype(jnp.bfloat16)
        to[tokens:end, :] = rows[:, compact]


def plane_sum(slots, keep, got, routes, from_x, from_y):
    half = from_x.shape[1]
    tokens = from_x.shape[0] - slots
    rows = both(keep, got, 0, slots // 2)
    me, ex, ey = (one_hot(routes[i * META : (i + 1) * META, :], slots) for i in range(3))
    mine = contract_rows(me, rows)
    left = from_x[0:tokens, :].astype(jnp.float32) + contract_rows(ey, from_y[tokens:, :])
    right = from_y[0:tokens, :].astype(jnp.float32) + contract_rows(ex, from_x[tokens:, :])
    return mine[:, 0:half] + left, mine[:, half:] + right


def plane_kernel(slots, keep, got, routes, from_x, from_y, *rest):
    total = rest[-1]
    half = from_x.shape[1]
    left, right = plane_sum(slots, keep, got, routes, from_x, from_y)
    for extra in rest[:-1]:
        left = left + extra[:, 0:half].astype(jnp.float32)
        right = right + extra[:, half:].astype(jnp.float32)
    total[:, 0:half] = left.astype(jnp.bfloat16)
    total[:, half:] = right.astype(jnp.bfloat16)


def last_kernel(slots, keep, got, routes, from_x, from_y, add_a, add_b, first, second, gain, who, out):
    half = from_x.shape[1]
    left, right = plane_sum(slots, keep, got, routes, from_x, from_y)
    total = jnp.concatenate([left, right], axis=1)
    total = total + add_a[...].astype(jnp.float32) + add_b[...].astype(jnp.float32)

    @pl.when(who[0] == 0)
    def _():
        out[...] = (second[...].astype(jnp.float32) - total).astype(jnp.bfloat16)

    @pl.when(who[0] != 0)
    def _():
        values = first[...].astype(jnp.float32)
        inverse = lax.rsqrt(jnp.mean(values * values, axis=1, keepdims=True) + EPSILON)
        normed_grad = total * gain[...].astype(jnp.float32)
        inner = jnp.mean(normed_grad * values, axis=1, keepdims=True)
        out[...] = (
            inverse * normed_grad - values * inverse * inverse * inverse * inner
        ).astype(jnp.bfloat16)


def call(kernel, name, outs, args, scalars=(), hbm=(), scratch=(), room=8):
    specs, args = [], list(args)
    for i in range(len(args)):
        if i in scalars:
            specs.append(pl.BlockSpec(memory_space=pltpu.SMEM))
        elif i in hbm:
            specs.append(pl.BlockSpec(memory_space=pl.ANY))
        else:
            args[i] = pltpu.with_memory_space_constraint(args[i], pltpu.VMEM)
            specs.append(pl.BlockSpec(memory_space=pltpu.VMEM))
    return pl.pallas_call(
        kernel,
        out_shape=[pltpu.VMEM(shape, dtype) for shape, dtype in outs],
        in_specs=specs,
        out_specs=[pl.BlockSpec(memory_space=pltpu.VMEM)] * len(outs),
        scratch_shapes=list(scratch),
        compiler_params=pltpu.CompilerParams(vmem_limit_bytes=room << 20),
        name=name,
    )(*args)


def dense_local(first_half, second_half, second_grad, norm_gain, expert_ids, gates, w_gate, w_up, w_down):
    tokens, width = first_half.shape
    half = width // 2
    owners = lax.axis_size("ep")
    replica = lax.axis_index("rep").astype(jnp.int32)
    place = lax.axis_index("ep").astype(jnp.int32)
    top = expert_ids.shape[1]
    slots = 5 * tokens * top // (4 * owners)
    portion = slots // 2
    plane = 4
    line = owners // plane
    bf16, f32 = jnp.bfloat16, jnp.float32

    def steps(move):
        pairs = [(i, move(i // plane)) for i in range(owners)]
        return [(i, to * plane + i % plane) for i, to in pairs if to is not None]

    across_x = [(i, i ^ 1) for i in range(owners)]
    across_y = [(i, i ^ 2) for i in range(owners)]
    pairs = steps(lambda z: z ^ 1)
    middle = steps({1: 2, 2: 1}.get)
    outward = steps({1: 0, 2: 3}.get)
    inward = steps({0: 1, 3: 2}.get)
    swap = [(0, 1), (1, 0)]

    def shift(value, route):
        return lax.ppermute(value, "ep", route)

    def other(value):
        return lax.ppermute(value, "rep", swap)

    z = place // plane
    is_middle = (z > 0) & (z < line - 1)
    who_rep = replica.reshape(1)
    who = jnp.stack([place, place ^ 1, place ^ 2, place ^ 3])
    gain = norm_gain.reshape(1, width)
    gate0, up0, down0 = w_gate[0], w_up[0], w_down[0]
    hidden_units = gate0.shape[1]

    with jax.named_scope("prologue"):
        (block,) = call(
            functools.partial(prologue_kernel, portion, slots),
            "prologue",
            [((tokens + META, width), bf16)],
            [first_half, second_grad, gain, expert_ids.T, gates.T, who_rep],
            scalars=(5,),
        )
    near = shift(block, pairs)
    mid_b = shift(block, middle)
    mid_c = shift(near, middle)
    end_b = shift(mid_b, outward)
    end_c = shift(mid_c, outward)
    gate1, up1, down1 = other(gate0), other(up0), other(down0)
    blocks = (
        block,
        near,
        jnp.where(is_middle, mid_b, end_b),
        jnp.where(is_middle, mid_c, end_c),
    )

    def dispatch(value):
        to_x, to_y, own, routes = call(
            functools.partial(pack_kernel, slots),
            "pack",
            [
                ((tokens + slots + META, half), bf16),
                ((tokens + slots + META, half), bf16),
                ((slots, width), bf16),
                ((3 * META, tokens), bf16),
            ],
            [value, who],
            scalars=(1,),
        )
        got_x, got_y = shift(to_x, across_x), shift(to_y, across_y)
        on_y, on_x, mine_x, mine_y = call(
            functools.partial(forward_kernel, slots),
            "forward",
            [((slots + META, half), bf16)] * 2 + [((slots, half), bf16)] * 2,
            [got_x, got_y],
        )
        by_y, by_x = shift(on_y, across_y), shift(on_x, across_x)
        keep, send = call(
            functools.partial(gather_kernel, slots),
            "gather",
            [((4 * portion, width), bf16)] * 2,
            [own, got_x, got_y, mine_x, mine_y, by_y, by_x],
        )
        return keep, other(send), routes, got_x, got_y, by_y

    def experts(keep, got, routes, got_x, got_y, by_y):
        rows = 4 * portion
        return call(
            expert_kernel,
            "experts",
            [
                ((rows, width), bf16),
                ((rows, width), bf16),
                ((8, tokens), f32),
                ((rows, width), bf16),
                ((rows, 2 * hidden_units), bf16),
            ],
            [keep, got, routes, got_x, got_y, by_y, who_rep, gate0, up0, down0, gate1, up1, down1],
            scalars=(6,),
            hbm=(7, 8, 9, 10, 11, 12),
            scratch=[
                pltpu.VMEM((width, hidden_units), bf16),
                pltpu.VMEM((width, hidden_units), bf16),
                pltpu.VMEM((hidden_units, width), bf16),
            ]
            * 2
            + [pltpu.SemaphoreType.DMA((6,))],
            room=24,
        )

    arrived = [dispatch(value) for value in blocks]
    solved = [experts(*a) for a in arrived]

    def give_back(a, s):
        keep, got = s[0], other(s[1])
        on_y, on_x = pl.pallas_call(
            corner_kernel,
            grid=(1,),
            out_shape=[jax.ShapeDtypeStruct((slots, half), bf16)] * 2,
            in_specs=[pl.BlockSpec((portion, width), lambda i: (3, 0))] * 2,
            out_specs=[pl.BlockSpec((slots, half), lambda i: (0, 0))] * 2,
            name="corner",
        )(keep, got)
        from_y, from_x = shift(on_y, across_y), shift(on_x, across_x)
        to_x, to_y = call(
            functools.partial(return_kernel, slots),
            "giveback",
            [((tokens + slots, half), bf16)] * 2,
            [keep, got, a[3], a[4], from_x, from_y],
        )
        return [keep, got, a[2], shift(to_x, across_x), shift(to_y, across_y)]

    def plane_total(parts, *extra):
        return call(
            functools.partial(plane_kernel, slots),
            "plane",
            [((tokens, width), bf16)],
            [*parts, *extra],
        )[0]

    def added(a, b):
        return (a.astype(f32) + b.astype(f32)).astype(bf16)

    total_c = plane_total(give_back(arrived[3], solved[3]))
    total_c = added(total_c, shift(total_c, inward))
    through_c = shift(total_c, middle)
    total_b = plane_total(give_back(arrived[2], solved[2]))
    total_b = added(total_b, shift(total_b, inward))
    through_b = shift(total_b, middle)
    total_a = plane_total(give_back(arrived[1], solved[1]), through_c)
    through_a = shift(total_a, pairs)
    parts = give_back(arrived[0], solved[0])
    (mine,) = call(
        functools.partial(last_kernel, slots),
        "last",
        [((tokens, width), bf16)],
        [*parts, through_a, through_b, first_half, second_half, gain, who_rep],
        scalars=(10,),
    )
    theirs = other(mine)
    is_first = replica == 0
    inverted = jnp.where(is_first, mine, theirs)
    first_grad = jnp.where(is_first, theirs, mine)

    scaled = jnp.concatenate([s[3] for s in solved], axis=0)
    hidden = jnp.concatenate([s[4] for s in solved], axis=0)
    down_theirs = contract_rows(hidden[:, hidden_units:], scaled)
    down_mine = contract_rows(hidden[:, :hidden_units], scaled) + other(down_theirs)
    w_down_grad = down_mine.astype(bf16)[None]

    factors = jnp.stack([s[2][:plane] for s in solved]).reshape(owners, tokens)
    target = jnp.arange(owners, dtype=jnp.int32)
    target_z = target // plane
    upper = z >= line // 2
    set_c = jnp.where(upper, 0, line - 1)
    set_b = jnp.where(upper, 1, line - 2)
    kind = jnp.where(
        target_z == z, 0, jnp.where(target_z == z ^ 1, 1, jnp.where(target_z == set_b, 2, 3))
    )
    del set_c
    source = kind * plane + (target % plane ^ place % plane)
    pick = source[:, None] == target[None, :]
    ordered = jnp.sum(jnp.where(pick[:, :, None], factors[None], 0.0), axis=1)
    by_expert = lax.all_to_all(ordered, "ep", split_axis=0, concat_axis=0, tiled=True)
    by_expert = by_expert + other(by_expert)
    asked = expert_ids[:, :, None] == jnp.arange(owners, dtype=jnp.int32)[None, None, :]
    gates_grad = jnp.sum(jnp.where(asked, by_expert.T[:, None, :], 0.0), axis=2)
    return (inverted, first_grad, gates_grad, w_down_grad)


def expert_pass(row_inputs, row_scaled, gate_mat, up_mat, down_mat):
    gate_pre = jnp.dot(row_inputs, gate_mat, preferred_element_type=jnp.float32)
    up_pre = jnp.dot(row_inputs, up_mat, preferred_element_type=jnp.float32)
    sigmoid_gate = jax.nn.sigmoid(gate_pre)
    swish_gate = gate_pre * sigmoid_gate
    hidden = (swish_gate * up_pre).astype(jnp.bfloat16)
    output = jnp.dot(hidden, down_mat, preferred_element_type=jnp.float32)
    hidden_grad = contract_cols(row_scaled, down_mat)
    gate_grad = (
        hidden_grad * up_pre * sigmoid_gate * (1.0 + gate_pre * (1.0 - sigmoid_gate))
    ).astype(jnp.bfloat16)
    up_grad = (hidden_grad * swish_gate).astype(jnp.bfloat16)
    input_grad = contract_cols(gate_grad, gate_mat) + contract_cols(up_grad, up_mat)
    return (output, input_grad, contract_rows(hidden, row_scaled))


def local(first_half, second_half, second_grad, norm_gain, expert_ids, gates, w_gate, w_up, w_down):
    token_count, model_width = first_half.shape
    top_count = expert_ids.shape[1]
    local_experts = w_gate.shape[0]
    owners = lax.axis_size("ep")
    replicas = lax.axis_size("rep")
    replica_index = lax.axis_index("rep")
    experts_all = local_experts * owners
    assigned = token_count * top_count
    capacity = 5 * token_count * top_count // (4 * experts_all)
    portion = capacity // replicas
    slots_all = experts_all * capacity
    slots_mine = experts_all * portion
    full_gate, full_up, full_down = (
        lax.all_gather(w_gate, "rep", axis=2, tiled=True),
        lax.all_gather(w_up, "rep", axis=2, tiled=True),
        lax.all_gather(w_down, "rep", axis=1, tiled=True),
    )
    expert_range = jnp.arange(experts_all, dtype=jnp.int32)
    hits = (expert_ids[:, :, None] == expert_range[None, None, :]).astype(jnp.bfloat16)
    incidence = jnp.sum(hits, axis=1)
    token_range = jnp.arange(token_count, dtype=jnp.int32)
    strictly_before = (token_range[:, None] > token_range[None, :]).astype(jnp.bfloat16)
    earlier = jnp.dot(strictly_before, incidence, preferred_element_type=jnp.float32)
    slot_rank = jnp.sum(hits.astype(jnp.float32) * earlier[:, None, :], axis=2).astype(jnp.int32)
    flat_ids = expert_ids.reshape(assigned)
    flat_rank = slot_rank.reshape(assigned)
    target = flat_ids * capacity + flat_rank
    local_rank = flat_rank - replica_index * portion
    is_mine = (local_rank >= 0) & (local_rank < portion)
    destination = jnp.where(is_mine, flat_ids * portion + local_rank, slots_mine)
    slot_source = (
        jnp.full((slots_mine,), assigned, jnp.int32)
        .at[destination]
        .set(jnp.arange(assigned, dtype=jnp.int32), mode="drop")
    )
    is_live = slot_source < assigned
    clamped = jnp.minimum(slot_source, assigned - 1)
    source_token = clamped // top_count
    values = first_half.astype(jnp.float32)
    inverse = lax.rsqrt(jnp.mean(values * values, axis=1, keepdims=True) + EPSILON)
    gain_value = norm_gain.astype(jnp.float32)
    normed = (values * inverse * gain_value).astype(jnp.bfloat16)
    flat_gates = gates.reshape(assigned)
    zero_half = jnp.zeros((), jnp.bfloat16)
    mine_inputs = jnp.where(is_live[:, None], normed[source_token], zero_half)
    slot_scaled = (
        flat_gates[clamped][:, None] * second_grad[source_token].astype(jnp.float32)
    ).astype(jnp.bfloat16)
    mine_scaled = jnp.where(is_live[:, None], slot_scaled, zero_half)
    got_inputs, got_scaled = (
        lax.all_to_all(mine_inputs, "ep", split_axis=0, concat_axis=0, tiled=True),
        lax.all_to_all(mine_scaled, "ep", split_axis=0, concat_axis=0, tiled=True),
    )
    grouped_inputs = got_inputs.reshape(owners, local_experts, portion, model_width)
    grouped_scaled = got_scaled.reshape(owners, local_experts, portion, model_width)
    out_list, grad_list, down_list = ([], [], [])
    row_inputs = grouped_inputs[:, 0].reshape(owners * portion, model_width)
    row_scaled = grouped_scaled[:, 0].reshape(owners * portion, model_width)
    output, input_grad, grad_down = expert_pass(
        row_inputs, row_scaled, full_gate[0], full_up[0], full_down[0]
    )
    out_list.append(output.astype(jnp.bfloat16).reshape(owners, 1, portion, model_width))
    grad_list.append(input_grad.astype(jnp.bfloat16).reshape(owners, 1, portion, model_width))
    down_list.append(grad_down)
    back_out = out_list[0].reshape(owners * local_experts * portion, model_width)
    back_grad = grad_list[0].reshape(owners * local_experts * portion, model_width)
    summed_down = lax.psum_scatter(jnp.stack(down_list), "rep", scatter_dimension=1, tiled=True)
    w_down_grad = summed_down.astype(jnp.bfloat16)
    returned_out, returned_grad = (
        lax.all_to_all(back_out, "ep", split_axis=0, concat_axis=0, tiled=True),
        lax.all_to_all(back_grad, "ep", split_axis=0, concat_axis=0, tiled=True),
    )
    whole_out, whole_grad = (
        lax.all_gather(
            returned_out.reshape(experts_all, portion, model_width), "rep", axis=1, tiled=True
        ),
        lax.all_gather(
            returned_grad.reshape(experts_all, portion, model_width), "rep", axis=1, tiled=True
        ),
    )
    whole_out = whole_out.reshape(slots_all, model_width)
    whole_grad = whole_grad.reshape(slots_all, model_width)
    out_rows = whole_out[target].reshape(token_count, top_count, model_width)
    grad_rows = whole_grad[target].reshape(token_count, top_count, model_width)
    inverted = (
        second_half.astype(jnp.float32)
        - jnp.sum(gates[:, :, None] * out_rows.astype(jnp.float32), axis=1)
    ).astype(jnp.bfloat16)
    gates_grad = jnp.einsum("td,tkd->tk", second_grad, out_rows, preferred_element_type=jnp.float32)
    normed_grad = jnp.sum(grad_rows.astype(jnp.float32), axis=1) * gain_value
    first_grad = (
        inverse * normed_grad
        - values
        * inverse
        * inverse
        * inverse
        * jnp.mean(normed_grad * values, axis=1, keepdims=True)
    ).astype(jnp.bfloat16)
    return (inverted, first_grad, gates_grad, w_down_grad)


def is_dense(mesh, args):
    first_half, expert_ids, w_gate = args[0], args[4], args[6]
    owners, replicas = mesh.shape["ep"], mesh.shape["rep"]
    tokens, width = first_half.shape[0] // owners, first_half.shape[1]
    experts, top = w_gate.shape[0], expert_ids.shape[1]
    slots = 5 * tokens * top // (4 * experts)
    fits = tokens % LANES == 0 and width == experts * tokens and slots % (8 * replicas) == 0
    return fits and experts == owners == 16 and replicas == 2 and 2 * top >= experts


def solution(mesh):
    def run(*args):
        body = dense_local if is_dense(mesh, args) else local
        return jax.shard_map(
            body,
            mesh=mesh,
            in_specs=(
                P("ep", None),
                P("ep", None),
                P("ep", None),
                P(),
                P("ep", None),
                P("ep", None),
                P("ep", None, "rep"),
                P("ep", None, "rep"),
                P("ep", "rep", None),
            ),
            out_specs=(P("ep", None), P("ep", None), P("ep", None), P("ep", "rep", None)),
            check_vma=False,
        )(*args)

    return run
```

```python
import functools

import jax
import jax.numpy as jnp
from jax import lax
from jax.experimental import pallas as pl
from jax.experimental.pallas import tpu as pltpu
from jax.sharding import PartitionSpec as P


EPSILON = 1e-06
META = 8
LANES = 128


def contract_rows(left, right):
    return lax.dot_general(
        left, right, (((0,), (0,)), ((), ())), preferred_element_type=jnp.float32
    )


def contract_cols(left, right):
    return lax.dot_general(
        left, right, (((1,), (1,)), ((), ())), preferred_element_type=jnp.float32
    )


def product(left, right):
    return jnp.dot(left, right, preferred_element_type=jnp.float32)


def chooser(tile, slots):
    code = tile[0:1, :].astype(jnp.float32)
    number = lax.broadcasted_iota(jnp.int32, (slots, code.shape[1]), 0).astype(jnp.float32)
    return number == code


def one_hot(tile, slots):
    return chooser(tile, slots).astype(jnp.float32).astype(jnp.bfloat16)


def gate_row(tile):
    parts = tile.astype(jnp.float32)
    return parts[1:2, :] + parts[2:3, :] + parts[3:4, :]


def wide(gain):
    rows = gain.astype(jnp.float32)
    return jnp.concatenate([rows[i : i + 1, :] for i in range(rows.shape[0])], axis=1)


def prologue_kernel(half, slots, first_in, grad_in, gain_in, ids_in, gates_in, who, block, first, gain, ids, gates, arrive):
    tokens = first.shape[0]
    replica = who[0]
    copies = [
        pltpu.make_async_copy(source, target, arrive.at[i])
        for i, (source, target) in enumerate(
            ((ids_in, ids), (gates_in, gates), (gain_in, gain), (first_in, first))
        )
    ]
    direct = pltpu.make_async_copy(grad_in, block.at[0:tokens, :], arrive.at[3])
    for copy in copies[0:3]:
        copy.start()

    @pl.when(replica == 0)
    def _():
        copies[3].start()

    @pl.when(replica != 0)
    def _():
        direct.start()

    for copy in copies[0:3]:
        copy.wait()
    experts = block.shape[1] // tokens
    expert = lax.broadcasted_iota(jnp.int32, (experts, tokens), 0)
    named = jnp.zeros((experts, tokens), jnp.float32)
    weight = jnp.zeros((experts, tokens), jnp.float32)
    for k in range(ids.shape[0]):
        hit = ids[k : k + 1, :] == expert
        named = named + jnp.where(hit, 1.0, 0.0)
        weight = weight + jnp.where(hit, gates[k : k + 1, :], 0.0)
    before = lax.broadcasted_iota(jnp.int32, (tokens, tokens), 0)
    after = lax.broadcasted_iota(jnp.int32, (tokens, tokens), 1)
    earlier = jnp.where(before < after, 1.0, 0.0).astype(jnp.bfloat16)
    rank = product(named.astype(jnp.bfloat16), earlier)
    rank = rank - (replica * half).astype(jnp.float32)
    rank = jnp.where(rank < 0.0, rank + slots, rank)
    code = jnp.where(named > 0.0, rank, -1.0)
    high = weight.astype(jnp.bfloat16).astype(jnp.float32)
    middle = (weight - high).astype(jnp.bfloat16).astype(jnp.float32)
    low = weight - high - middle
    line = lax.broadcasted_iota(jnp.int32, (META, tokens), 0)
    for e in range(experts):
        tile = jnp.where(line == 0, code[e : e + 1, :], 0.0)
        tile = jnp.where(line == 1, high[e : e + 1, :], tile)
        tile = jnp.where(line == 2, middle[e : e + 1, :], tile)
        tile = jnp.where(line == 3, low[e : e + 1, :], tile)
        block[tokens : tokens + META, e * tokens : (e + 1) * tokens] = tile.astype(jnp.bfloat16)

    @pl.when(replica == 0)
    def _():
        copies[3].wait()
        values = first[...].astype(jnp.float32)
        inverse = lax.rsqrt(jnp.mean(values * values, axis=1, keepdims=True) + EPSILON)
        block[0:tokens, :] = (values * inverse * wide(gain[...])).astype(jnp.bfloat16)

    @pl.when(replica != 0)
    def _():
        direct.wait()


def pack_kernel(slots, block, who, to_x, to_y, own, routes):
    tokens = block.shape[0] - META
    half = block.shape[1] // 2
    end = tokens + slots

    def tile_of(place):
        start = pl.multiple_of(who[place] * tokens, LANES)
        return block[tokens : tokens + META, pl.ds(start, tokens)]

    me, ex, ey, ed = (tile_of(place) for place in range(4))
    for to, nearby, dense, compact in (
        (to_x, ex, slice(0, half), slice(half, 2 * half)),
        (to_y, ey, slice(half, 2 * half), slice(0, half)),
    ):
        to[0:tokens, :] = block[0:tokens, dense]
        taken = product(one_hot(nearby, slots), block[0:tokens, compact])
        to[tokens:end, :] = taken.astype(jnp.bfloat16)
        to[end : end + META, :] = jnp.zeros((META, half), jnp.bfloat16)
        to[end : end + META, 0:tokens] = nearby
        to[end : end + META, tokens : 2 * tokens] = ed
    own[...] = product(one_hot(me, slots), block[0:tokens, :]).astype(jnp.bfloat16)
    routes[0:META, :] = me
    routes[META : 2 * META, :] = ex
    routes[2 * META : 3 * META, :] = ey


def choose_kernel(slots, near, far, who, to_x, to_y, own, routes, block):
    block[...] = jnp.where(who[4] != 0, near[...], far[...])
    pack_kernel(slots, block, who, to_x, to_y, own, routes)


def forward_kernel(slots, got_x, got_y, on_y, on_x, mine_x, mine_y, routes):
    tokens = got_x.shape[0] - slots - META
    end = tokens + slots
    half = got_x.shape[1]
    for i, (got, on, mine) in enumerate(((got_x, on_y, mine_x), (got_y, on_x, mine_y))):
        me = got[end : end + META, 0:tokens]
        other = got[end : end + META, tokens : 2 * tokens]
        rows = got[0:tokens, :]
        on[0:slots, :] = product(one_hot(other, slots), rows).astype(jnp.bfloat16)
        on[slots : slots + META, :] = jnp.zeros((META, half), jnp.bfloat16)
        on[slots : slots + META, 0:tokens] = other
        mine[...] = product(one_hot(me, slots), rows).astype(jnp.bfloat16)
        routes[2 * i * META : (2 * i + 1) * META, :] = me
        routes[(2 * i + 1) * META : (2 * i + 2) * META, :] = other


def gather_kernel(slots, own, got_x, got_y, mine_x, mine_y, by_y, by_x, keep, send, route):
    portion = slots // 2
    tokens = got_x.shape[0] - slots - META
    half = got_x.shape[1]
    for base, out in ((0, keep), (portion, send)):
        rows = slice(base, base + portion)
        late = slice(tokens + base, tokens + base + portion)
        out[0:portion, :] = own[rows, :]
        out[portion : 2 * portion, 0:half] = mine_x[rows, :]
        out[portion : 2 * portion, half:] = got_x[late, :]
        out[2 * portion : 3 * portion, 0:half] = got_y[late, :]
        out[2 * portion : 3 * portion, half:] = mine_y[rows, :]
        out[3 * portion : 4 * portion, 0:half] = by_y[rows, :]
        out[3 * portion : 4 * portion, half:] = by_x[rows, :]
    route[...] = by_y[slots : slots + META, 0:tokens]


def hold_kernel(g0, u0, d0, g1, u1, d1, gate_mat, up_mat, down_mat, arrive):
    part = g0.shape[1]
    copies = [
        pltpu.make_async_copy(source, target, arrive.at[i])
        for i, (source, target) in enumerate(
            (
                (g0, gate_mat.at[:, 0:part]),
                (g1, gate_mat.at[:, part : 2 * part]),
                (u0, up_mat.at[:, 0:part]),
                (u1, up_mat.at[:, part : 2 * part]),
                (d0, down_mat.at[0:part, :]),
                (d1, down_mat.at[part : 2 * part, :]),
            )
        )
    ]
    for copy in copies:
        copy.start()
    for copy in copies:
        copy.wait()


def expert_kernel(
    keep, got, near, sides, route, gate_mat, up_mat, down_mat, who,
    keep_out, send_out, factor, scaled_out, hidden_out,
):
    portion = keep.shape[0] // 4
    tokens = near.shape[1]
    is_first = who[0] == 0
    inputs = jnp.where(is_first, keep[...], got[...])
    grads = jnp.where(is_first, got[...], keep[...])
    tiles = (near[0:META, :], sides[0:META, :], sides[2 * META : 3 * META, :], route[...])
    choices = [chooser(tile, portion) for tile in tiles]
    gate = jnp.concatenate(
        [
            jnp.sum(jnp.where(c, gate_row(tile), 0.0), axis=1, keepdims=True)
            for c, tile in zip(choices, tiles)
        ],
        axis=0,
    )
    scaled = (gate * grads.astype(jnp.float32)).astype(jnp.bfloat16)
    scaled_out[...] = scaled
    gate_pre = product(inputs, gate_mat[...])
    up_pre = product(inputs, up_mat[...])
    sigmoid_gate = jax.nn.sigmoid(gate_pre)
    swish_gate = gate_pre * sigmoid_gate
    hidden = (swish_gate * up_pre).astype(jnp.bfloat16)
    hidden_out[...] = hidden
    hidden_grad = contract_cols(scaled, down_mat[...])
    gate_grad = (
        hidden_grad * up_pre * sigmoid_gate * (1.0 + gate_pre * (1.0 - sigmoid_gate))
    ).astype(jnp.bfloat16)
    up_grad = (hidden_grad * swish_gate).astype(jnp.bfloat16)
    output = product(hidden, down_mat[...])
    input_grad = contract_cols(gate_grad, gate_mat[...]) + contract_cols(up_grad, up_mat[...])
    rounded = output.astype(jnp.bfloat16).astype(jnp.float32)
    inner = jnp.sum(grads.astype(jnp.float32) * rounded, axis=1, keepdims=True)
    weighted = (gate * rounded).astype(jnp.bfloat16)
    rounded_grad = input_grad.astype(jnp.bfloat16)
    keep_out[...] = jnp.where(is_first, weighted, rounded_grad)
    send_out[...] = jnp.where(is_first, rounded_grad, weighted)
    line = lax.broadcasted_iota(jnp.int32, (META, tokens), 0)
    for i, choice in enumerate(choices):
        part = inner[i * portion : (i + 1) * portion, :]
        row = jnp.sum(jnp.where(choice, part, 0.0), axis=0, keepdims=True)
        high = row.astype(jnp.bfloat16).astype(jnp.float32)
        tile = jnp.where(line == 0, high, jnp.where(line == 1, row - high, 0.0))
        factor[i * META : (i + 1) * META, :] = tile.astype(jnp.bfloat16)


def down_kernel(portion, *refs):
    sets, rest = (len(refs) - 1) // 2, refs[-2]
    start = portion
    out = refs[-1]
    hidden = jnp.concatenate([r[:, start : start + out.shape[0]] for r in refs[0:sets]], axis=0)
    scaled = jnp.concatenate([r[...] for r in refs[sets : 2 * sets]], axis=0)
    total = contract_rows(hidden, scaled)
    if len(refs) == 2 * sets + 2:
        total = total + rest[...]
    out[...] = total.astype(out.dtype)


def both(keep, got, number, portion):
    rows = slice(number * portion, (number + 1) * portion)
    return jnp.concatenate([keep[rows, :], got[rows, :]], axis=0)


def corner_kernel(keep, got, factor, on_y, on_x):
    half = on_y.shape[1]
    slots = on_x.shape[0]
    tokens = factor.shape[1]
    rows = both(keep, got, 3, slots // 2)
    on_y[0:slots, :] = rows[:, 0:half]
    on_y[slots:, :] = jnp.zeros((META, half), jnp.bfloat16)
    on_y[slots:, 0:tokens] = factor[3 * META : 4 * META, :]
    on_x[...] = rows[:, half:]


def return_kernel(slots, keep, got, sides, from_x, from_y, factor, to_x, to_y):
    half = to_x.shape[1]
    tokens = to_x.shape[0] - slots - META
    end = tokens + slots
    for number, corner, to, dense, compact in (
        (1, from_y, to_x, slice(0, half), slice(half, 2 * half)),
        (2, from_x, to_y, slice(half, 2 * half), slice(0, half)),
    ):
        rows = both(keep, got, number, slots // 2)
        line = 2 * (number - 1) * META
        me, other = sides[line : line + META, :], sides[line + META : line + 2 * META, :]
        total = contract_rows(one_hot(me, slots), rows[:, dense])
        total = total + contract_rows(one_hot(other, slots), corner[0:slots, :])
        to[0:tokens, :] = total.astype(jnp.bfloat16)
        to[tokens:end, :] = rows[:, compact]
        to[end : end + META, :] = jnp.zeros((META, half), jnp.bfloat16)
        to[end : end + META, 0:tokens] = factor[number * META : (number + 1) * META, :]
    to_x[end : end + META, tokens : 2 * tokens] = from_y[slots : slots + META, 0:tokens]


def plane_sum(slots, keep, got, routes, from_x, from_y):
    half = from_x.shape[1]
    tokens = from_x.shape[0] - slots - META
    end = tokens + slots
    rows = both(keep, got, 0, slots // 2)
    me, ex, ey = (one_hot(routes[i * META : (i + 1) * META, :], slots) for i in range(3))
    mine = contract_rows(me, rows)
    left = from_x[0:tokens, :].astype(jnp.float32) + contract_rows(ey, from_y[tokens:end, :])
    right = from_y[0:tokens, :].astype(jnp.float32) + contract_rows(ex, from_x[tokens:end, :])
    return mine[:, 0:half] + left, mine[:, half:] + right


def place_factors(who, from_x, from_y, factor, out):
    tokens = factor.shape[1]
    end = from_x.shape[0] - META
    out[...] = jnp.zeros(out.shape, jnp.bfloat16)
    for place, tile in (
        (0, factor[0:META, :]),
        (1, from_x[end : end + META, 0:tokens]),
        (2, from_y[end : end + META, 0:tokens]),
        (3, from_x[end : end + META, tokens : 2 * tokens]),
    ):
        out[:, pl.ds(pl.multiple_of(who[place] * tokens, LANES), tokens)] = tile


def plane_kernel(slots, keep, got, routes, from_x, from_y, factor, who, *rest):
    *outs, spread = rest
    half = from_x.shape[1]
    tokens = from_x.shape[0] - slots - META
    place_factors(who, from_x, from_y, factor, spread)
    sums = plane_sum(slots, keep, got, routes, from_x, from_y)
    for i, total in enumerate(sums):
        out, start = (outs[i], 0) if len(outs) == 2 else (outs[0], i * half)
        out[0:tokens, start : start + half] = total.astype(jnp.bfloat16)
        out[tokens:, start : start + half] = spread[:, i * half : (i + 1) * half]


def add_kernel(left, right, out):
    out[...] = (left[...].astype(jnp.float32) + right[...].astype(jnp.float32)).astype(jnp.bfloat16)


def last_kernel(slots, keep, got, routes, from_x, from_y, factor, near, far, b0, b1, first, second, gain, ids, who, role, out, spread):
    half = from_x.shape[1]
    tokens = first.shape[0]
    place_factors(who, from_x, from_y, factor, spread)
    sums, tails = [], []
    for i, (total, b) in enumerate(
        zip(plane_sum(slots, keep, got, routes, from_x, from_y), (b0, b1))
    ):
        lanes = slice(i * half, (i + 1) * half)
        passed = near[:, lanes].astype(jnp.float32) + far[:, lanes].astype(jnp.float32)
        passed = passed + b[...].astype(jnp.float32)
        sums.append(total + passed[0:tokens, :])
        tails.append(passed[tokens:, :] + spread[:, lanes].astype(jnp.float32))
    total = jnp.concatenate(sums, axis=1)
    tail = jnp.concatenate(tails, axis=1)
    factors = tail[0:1, :] + tail[1:2, :]
    asked = ids[...]
    picked = jnp.zeros(asked.shape, jnp.float32)
    for e in range(factors.shape[1] // tokens):
        picked = picked + jnp.where(asked == e, factors[:, e * tokens : (e + 1) * tokens], 0.0)
    high = picked.astype(jnp.bfloat16)
    out[tokens:, :] = jnp.zeros((META, 2 * half), jnp.bfloat16)
    out[tokens:, 0:tokens] = high
    out[tokens:, tokens : 2 * tokens] = (picked - high.astype(jnp.float32)).astype(jnp.bfloat16)

    @pl.when(role[0] == 0)
    def _():
        out[0:tokens, :] = (second[...].astype(jnp.float32) - total).astype(jnp.bfloat16)

    @pl.when(role[0] != 0)
    def _():
        values = first[...].astype(jnp.float32)
        inverse = lax.rsqrt(jnp.mean(values * values, axis=1, keepdims=True) + EPSILON)
        normed_grad = total * wide(gain[...])
        inner = jnp.mean(normed_grad * values, axis=1, keepdims=True)
        out[0:tokens, :] = (
            inverse * normed_grad - values * inverse * inverse * inverse * inner
        ).astype(jnp.bfloat16)


def finish_kernel(mine, theirs, who, inverted, first_grad, gates_out, arrive):
    tokens = inverted.shape[0]

    def write(a, b):
        copies = [
            pltpu.make_async_copy(a.at[0:tokens, :], inverted, arrive.at[0]),
            pltpu.make_async_copy(b.at[0:tokens, :], first_grad, arrive.at[1]),
        ]
        for copy in copies:
            copy.start()
        for copy in copies:
            copy.wait()

    @pl.when(who[0] == 0)
    def _():
        write(mine, theirs)

    @pl.when(who[0] != 0)
    def _():
        write(theirs, mine)

    tails = [r[tokens:, 0 : 2 * tokens].astype(jnp.float32) for r in (mine, theirs)]
    total = tails[0] + tails[1]
    gates_out[...] = total[:, 0:tokens] + total[:, tokens:]


def call(kernel, outs, args, scalars=(), plain=(), place_any=False, scratch=(), room=4):
    specs, args = [], list(args)
    for i in range(len(args)):
        if i in scalars:
            specs.append(pl.BlockSpec(memory_space=pltpu.SMEM))
        else:
            if i not in plain and not place_any:
                args[i] = pltpu.with_memory_space_constraint(args[i], pltpu.VMEM)
            specs.append(pl.BlockSpec(memory_space=pl.ANY if place_any else pltpu.VMEM))
    return pl.pallas_call(
        kernel,
        out_shape=[pltpu.VMEM(shape, dtype) for shape, dtype in outs],
        in_specs=specs,
        out_specs=[pl.BlockSpec(memory_space=pltpu.VMEM)] * len(outs),
        scratch_shapes=list(scratch),
        compiler_params=pltpu.CompilerParams(vmem_limit_bytes=room << 20),
    )(*args)


def dense_local(*args):
    return dense_body(*args)


def dense_body(first_half, second_half, second_grad, norm_gain, expert_ids, gates, w_gate, w_up, w_down):
    tokens, width = first_half.shape
    half = width // 2
    owners = lax.axis_size("ep")
    replica = lax.axis_index("rep").astype(jnp.int32)
    place = lax.axis_index("ep").astype(jnp.int32)
    top = expert_ids.shape[1]
    slots = 5 * tokens * top // (4 * owners)
    portion = slots // 2
    plane = 4
    line = owners // plane
    bf16, f32 = jnp.bfloat16, jnp.float32

    def steps(move):
        pairs = [(i, move(i // plane)) for i in range(owners)]
        return [(i, to * plane + i % plane) for i, to in pairs if to is not None]

    across_x = [(i, i ^ 1) for i in range(owners)]
    across_y = [(i, i ^ 2) for i in range(owners)]
    pairs = steps(lambda z: z ^ 1)
    middle = steps({1: 2, 2: 1}.get)
    outward = steps({1: 0, 2: 3}.get)
    inward = steps({0: 1, 3: 2}.get)
    distant = steps({1: 3, 2: 0}.get)

    def shift(value, route):
        return lax.ppermute(value, "ep", route)

    def other(value):
        return lax.ppermute(value, "rep", [(0, 1), (1, 0)])

    z = place // plane
    is_middle = ((z > 0) & (z < line - 1)).astype(jnp.int32)
    role = replica.reshape(1)
    who = jnp.stack([place, place ^ 1, place ^ 2, place ^ 3, is_middle])
    gain = norm_gain.reshape(width // LANES, LANES)
    gate0, up0, down0 = w_gate[0], w_up[0], w_down[0]
    hidden_units = gate0.shape[1]
    ids = expert_ids.T

    (block,) = call(
        functools.partial(prologue_kernel, portion, slots),
        [((tokens + META, width), bf16)],
        [first_half, second_grad, gain, ids, gates.T, role],
        scalars=(5,),
        place_any=True,
        scratch=[
            pltpu.VMEM((tokens, width), bf16),
            pltpu.VMEM((width // LANES, LANES), bf16),
            pltpu.VMEM((top, tokens), jnp.int32),
            pltpu.VMEM((top, tokens), f32),
            pltpu.SemaphoreType.DMA((4,)),
        ],
    )
    near = shift(block, pairs)
    mid_b = shift(block, middle)
    mid_c = shift(near, middle)
    end_b = shift(mid_b, outward)
    end_c = shift(mid_c, outward)
    gate1, up1, down1 = other(gate0), other(up0), other(down0)

    gate_mat, up_mat, down_mat = call(
        hold_kernel,
        [((width, 2 * hidden_units), bf16)] * 2 + [((2 * hidden_units, width), bf16)],
        [gate0, up0, down0, gate1, up1, down1],
        place_any=True,
        scratch=[pltpu.SemaphoreType.DMA((6,))],
    )

    def dispatch(value, value_far=None):
        args = [value] if value_far is None else [value, value_far]
        to_x, to_y, own, near_routes = call(
            functools.partial(pack_kernel if value_far is None else choose_kernel, slots),
            [
                ((tokens + slots + META, half), bf16),
                ((tokens + slots + META, half), bf16),
                ((slots, width), bf16),
                ((3 * META, tokens), bf16),
            ],
            [*args, who],
            scalars=(len(args),),
            scratch=[pltpu.VMEM((tokens + META, width), bf16)] if len(args) == 2 else [],
        )
        got_x, got_y = shift(to_x, across_x), shift(to_y, across_y)
        on_y, on_x, mine_x, mine_y, sides = call(
            functools.partial(forward_kernel, slots),
            [((slots + META, half), bf16)] * 2
            + [((slots, half), bf16)] * 2
            + [((4 * META, tokens), bf16)],
            [got_x, got_y],
        )
        by_y, by_x = shift(on_y, across_y), shift(on_x, across_x)
        keep, send, route = call(
            functools.partial(gather_kernel, slots),
            [((4 * portion, width), bf16)] * 2 + [((META, tokens), bf16)],
            [own, got_x, got_y, mine_x, mine_y, by_y, by_x],
        )
        return keep, other(send), near_routes, sides, route

    def experts(keep, got, near_routes, sides, route):
        rows = 4 * portion
        return call(
            expert_kernel,
            [
                ((rows, width), bf16),
                ((rows, width), bf16),
                ((4 * META, tokens), bf16),
                ((rows, width), bf16),
                ((rows, 2 * hidden_units), bf16),
            ],
            [keep, got, near_routes, sides, route, gate_mat, up_mat, down_mat, role],
            scalars=(8,),
            room=12,
        )

    arrived = [dispatch(block), dispatch(near), dispatch(mid_b, end_b), dispatch(mid_c, end_c)]
    solved = [experts(*a) for a in arrived]

    def give_back(i):
        keep, factor, got = solved[i][0], solved[i][2], other(solved[i][1])
        on_y, on_x = call(
            corner_kernel,
            [((slots + META, half), bf16), ((slots, half), bf16)],
            [keep, got, factor],
        )
        from_y, from_x = shift(on_y, across_y), shift(on_x, across_x)
        to_x, to_y = call(
            functools.partial(return_kernel, slots),
            [((tokens + slots + META, half), bf16)] * 2,
            [keep, got, arrived[i][3], from_x, from_y, factor],
        )
        got_x, got_y = shift(to_x, across_x), shift(to_y, across_y)
        return [keep, got, arrived[i][2], got_x, got_y, factor]

    def plane_total(i, cuts=1):
        return call(
            functools.partial(plane_kernel, slots),
            [((tokens + META, width // cuts), bf16)] * cuts,
            [*give_back(i), who],
            scalars=(6,),
            scratch=[pltpu.VMEM((META, width), bf16)],
        )

    def met(total):
        passed = shift(total, inward)
        return call(add_kernel, [(total.shape, bf16)], [total, passed])[0]

    through_a = shift(plane_total(1)[0], pairs)
    through_c = shift(met(plane_total(3)[0]), distant)
    through_b = [shift(met(total), middle) for total in plane_total(2, 2)]
    first_late, second_late, gain_late, ids_late = lax.optimization_barrier(
        (first_half, second_half, gain, ids, block)
    )[:4]
    (mine,) = call(
        functools.partial(last_kernel, slots),
        [((tokens + META, width), bf16)],
        [*give_back(0), through_a, through_c, *through_b]
        + [first_late, second_late, gain_late, ids_late, who, role],
        scalars=(14, 15),
        scratch=[pltpu.VMEM((META, width), bf16)],
        room=8,
    )
    inverted, first_grad, by_choice = pl.pallas_call(
        finish_kernel,
        out_shape=[jax.ShapeDtypeStruct((tokens, width), bf16)] * 2
        + [jax.ShapeDtypeStruct((top, tokens), f32)],
        in_specs=[pl.BlockSpec(memory_space=pltpu.VMEM)] * 2
        + [pl.BlockSpec(memory_space=pltpu.SMEM)],
        out_specs=[pl.BlockSpec(memory_space=pl.ANY)] * 2
        + [pl.BlockSpec(memory_space=pltpu.VMEM)],
        scratch_shapes=[pltpu.SemaphoreType.DMA((2,))],
        compiler_params=pltpu.CompilerParams(vmem_limit_bytes=4 << 20),
        name="finish",
    )(
        pltpu.with_memory_space_constraint(mine, pltpu.VMEM),
        pltpu.with_memory_space_constraint(other(mine), pltpu.VMEM),
        role,
    )
    gates_grad = by_choice.T

    rows = [s[4] for s in solved] + [s[3] for s in solved]
    shape = (hidden_units, width)
    (down_theirs,) = call(
        functools.partial(down_kernel, hidden_units), [(shape, f32)], rows, room=12
    )
    (down_mine,) = call(
        functools.partial(down_kernel, 0), [(shape, bf16)], [*rows, other(down_theirs)], room=12
    )
    return (inverted, first_grad, gates_grad, down_mine[None])


def expert_pass(row_inputs, row_scaled, gate_mat, up_mat, down_mat):
    gate_pre = jnp.dot(row_inputs, gate_mat, preferred_element_type=jnp.float32)
    up_pre = jnp.dot(row_inputs, up_mat, preferred_element_type=jnp.float32)
    sigmoid_gate = jax.nn.sigmoid(gate_pre)
    swish_gate = gate_pre * sigmoid_gate
    hidden = (swish_gate * up_pre).astype(jnp.bfloat16)
    output = jnp.dot(hidden, down_mat, preferred_element_type=jnp.float32)
    hidden_grad = contract_cols(row_scaled, down_mat)
    gate_grad = (
        hidden_grad * up_pre * sigmoid_gate * (1.0 + gate_pre * (1.0 - sigmoid_gate))
    ).astype(jnp.bfloat16)
    up_grad = (hidden_grad * swish_gate).astype(jnp.bfloat16)
    input_grad = contract_cols(gate_grad, gate_mat) + contract_cols(up_grad, up_mat)
    return (output, input_grad, contract_rows(hidden, row_scaled))


def local(first_half, second_half, second_grad, norm_gain, expert_ids, gates, w_gate, w_up, w_down):
    token_count, model_width = first_half.shape
    top_count = expert_ids.shape[1]
    local_experts = w_gate.shape[0]
    owners = lax.axis_size("ep")
    replicas = lax.axis_size("rep")
    replica_index = lax.axis_index("rep")
    experts_all = local_experts * owners
    assigned = token_count * top_count
    capacity = 5 * token_count * top_count // (4 * experts_all)
    portion = capacity // replicas
    slots_all = experts_all * capacity
    slots_mine = experts_all * portion
    full_gate, full_up, full_down = (
        lax.all_gather(w_gate, "rep", axis=2, tiled=True),
        lax.all_gather(w_up, "rep", axis=2, tiled=True),
        lax.all_gather(w_down, "rep", axis=1, tiled=True),
    )
    expert_range = jnp.arange(experts_all, dtype=jnp.int32)
    hits = (expert_ids[:, :, None] == expert_range[None, None, :]).astype(jnp.bfloat16)
    incidence = jnp.sum(hits, axis=1)
    token_range = jnp.arange(token_count, dtype=jnp.int32)
    strictly_before = (token_range[:, None] > token_range[None, :]).astype(jnp.bfloat16)
    earlier = jnp.dot(strictly_before, incidence, preferred_element_type=jnp.float32)
    slot_rank = jnp.sum(hits.astype(jnp.float32) * earlier[:, None, :], axis=2).astype(jnp.int32)
    flat_ids = expert_ids.reshape(assigned)
    flat_rank = slot_rank.reshape(assigned)
    target = flat_ids * capacity + flat_rank
    local_rank = flat_rank - replica_index * portion
    is_mine = (local_rank >= 0) & (local_rank < portion)
    destination = jnp.where(is_mine, flat_ids * portion + local_rank, slots_mine)
    slot_source = (
        jnp.full((slots_mine,), assigned, jnp.int32)
        .at[destination]
        .set(jnp.arange(assigned, dtype=jnp.int32), mode="drop")
    )
    is_live = slot_source < assigned
    clamped = jnp.minimum(slot_source, assigned - 1)
    source_token = clamped // top_count
    values = first_half.astype(jnp.float32)
    inverse = lax.rsqrt(jnp.mean(values * values, axis=1, keepdims=True) + EPSILON)
    gain_value = norm_gain.astype(jnp.float32)
    normed = (values * inverse * gain_value).astype(jnp.bfloat16)
    flat_gates = gates.reshape(assigned)
    zero_half = jnp.zeros((), jnp.bfloat16)
    mine_inputs = jnp.where(is_live[:, None], normed[source_token], zero_half)
    slot_scaled = (
        flat_gates[clamped][:, None] * second_grad[source_token].astype(jnp.float32)
    ).astype(jnp.bfloat16)
    mine_scaled = jnp.where(is_live[:, None], slot_scaled, zero_half)
    got_inputs, got_scaled = (
        lax.all_to_all(mine_inputs, "ep", split_axis=0, concat_axis=0, tiled=True),
        lax.all_to_all(mine_scaled, "ep", split_axis=0, concat_axis=0, tiled=True),
    )
    grouped_inputs = got_inputs.reshape(owners, local_experts, portion, model_width)
    grouped_scaled = got_scaled.reshape(owners, local_experts, portion, model_width)
    out_list, grad_list, down_list = ([], [], [])
    row_inputs = grouped_inputs[:, 0].reshape(owners * portion, model_width)
    row_scaled = grouped_scaled[:, 0].reshape(owners * portion, model_width)
    output, input_grad, grad_down = expert_pass(
        row_inputs, row_scaled, full_gate[0], full_up[0], full_down[0]
    )
    out_list.append(output.astype(jnp.bfloat16).reshape(owners, 1, portion, model_width))
    grad_list.append(input_grad.astype(jnp.bfloat16).reshape(owners, 1, portion, model_width))
    down_list.append(grad_down)
    back_out = out_list[0].reshape(owners * local_experts * portion, model_width)
    back_grad = grad_list[0].reshape(owners * local_experts * portion, model_width)
    summed_down = lax.psum_scatter(jnp.stack(down_list), "rep", scatter_dimension=1, tiled=True)
    w_down_grad = summed_down.astype(jnp.bfloat16)
    returned_out, returned_grad = (
        lax.all_to_all(back_out, "ep", split_axis=0, concat_axis=0, tiled=True),
        lax.all_to_all(back_grad, "ep", split_axis=0, concat_axis=0, tiled=True),
    )
    whole_out, whole_grad = (
        lax.all_gather(
            returned_out.reshape(experts_all, portion, model_width), "rep", axis=1, tiled=True
        ),
        lax.all_gather(
            returned_grad.reshape(experts_all, portion, model_width), "rep", axis=1, tiled=True
        ),
    )
    whole_out = whole_out.reshape(slots_all, model_width)
    whole_grad = whole_grad.reshape(slots_all, model_width)
    out_rows = whole_out[target].reshape(token_count, top_count, model_width)
    grad_rows = whole_grad[target].reshape(token_count, top_count, model_width)
    inverted = (
        second_half.astype(jnp.float32)
        - jnp.sum(gates[:, :, None] * out_rows.astype(jnp.float32), axis=1)
    ).astype(jnp.bfloat16)
    gates_grad = jnp.einsum("td,tkd->tk", second_grad, out_rows, preferred_element_type=jnp.float32)
    normed_grad = jnp.sum(grad_rows.astype(jnp.float32), axis=1) * gain_value
    first_grad = (
        inverse * normed_grad
        - values
        * inverse
        * inverse
        * inverse
        * jnp.mean(normed_grad * values, axis=1, keepdims=True)
    ).astype(jnp.bfloat16)
    return (inverted, first_grad, gates_grad, w_down_grad)


def is_dense(mesh, args):
    first_half, expert_ids, w_gate = args[0], args[4], args[6]
    owners, replicas = mesh.shape["ep"], mesh.shape["rep"]
    tokens, width = first_half.shape[0] // owners, first_half.shape[1]
    experts, top = w_gate.shape[0], expert_ids.shape[1]
    slots = 5 * tokens * top // (4 * experts)
    fits = tokens % LANES == 0 and width == experts * tokens and slots % (8 * replicas) == 0
    return fits and experts == owners == 16 and replicas == 2 and 2 * top >= experts


def solution(mesh):
    def run(*args):
        dense = is_dense(mesh, args)
        step = jax.shard_map(
            dense_local if dense else local,
            mesh=mesh,
            in_specs=(
                P("ep", None),
                P("ep", None),
                P("ep", None),
                P(),
                P("ep", None),
                P("ep", None),
                P("ep", None, "rep"),
                P("ep", None, "rep"),
                P("ep", "rep", None),
            ),
            out_specs=(P("ep", None), P("ep", None), P("ep", None), P("ep", "rep", None)),
            check_vma=False,
        )
        return step(*args)

    return run
```
